32 devices in a mesh: req: 8 (over z, y), kvh: 2 (over x), ffn: 2 (over core).
Axes of the slice: x: 2, y: 2, z: 4, core: 2. Of those that a mesh axis runs over, the one named last changes fastest.
Arguments:
- queries: bfloat16 [8, 64, 8192], P('req', None, 'kvh'), may hold values from -8 to 8
- tree_keys: bfloat16 [8, 64, 1024], P('req', None, 'kvh'), may hold values from -4.5 to 4.5
- tree_token_values: bfloat16 [8, 64, 1024], P('req', None, 'kvh'), may hold values from -6 to 6
- cache_keys: bfloat16 [8, 8, 8192, 128], P('req', 'kvh', 'ffn'), may hold values from -4.5 to 4.5
- cached_value_rows: bfloat16 [8, 8, 8192, 128], P('req', 'kvh', 'ffn'), may hold values from -6 to 6
- lengths: int32 [8], replicated, may hold values from 1 to 8192, 16384 in all
- parents: int32 [8, 64], P('req'), may hold values from 0 to 63, as said below
- residual: float32 [512, 8192], P(('req', 'ffn'), 'kvh'), may hold values from -6 to 6
- out_weight: bfloat16 [8192, 8192], P('kvh', ('req', 'ffn')), may hold values from -0.0625 to 0.0625
- norm_gain: float32 [8192], P('kvh'), may hold values from 0.25 to 1.75
- gate_weight: bfloat16 [8192, 28672], P('kvh', ('req', 'ffn')), may hold values from -0.0625 to 0.0625
- up_weight: bfloat16 [8192, 28672], P('kvh', ('req', 'ffn')), may hold values from -0.0625 to 0.0625
- down_weight: bfloat16 [28672, 8192], P(('req', 'ffn'), 'kvh'), may hold values from -0.03125 to 0.03125
Outputs:
- layer_output: float32 [512, 8192], P(('req', 'ffn'), 'kvh')
The draws below stay inside these ranges and needn't reach their ends.
Inputs may be any that keep to these rules, and one draw needn't show every extreme that they name: parents[r, 0] = 0, and parents[r, i] < i for every node i > 0. The lengths of all requests sum to 16384, and the largest is exactly 8192.
All inputs are finite; a program needn't handle non-finite values.
Results may differ from the reference program's by a relative error of at most 0.003.
Values may be sent and summed in bfloat16 or wider, within the bound.
A program may use at most 128 MiB of HBM per device.

```python
import math
import jax
import jax.numpy as jnp
import numpy as np
from jax import lax

D = 8192
FF = 28672
QUERY_HEADS = 64
KEY_VALUE_HEADS = 8
HEAD_DIMENSION = 128
TREE_NODES = 64
CACHE_SLOTS = 8192
REQUEST_COUNT = 8
TOKENS = 512


def sign_layout(key):
    random_bits = jax.random.randint(jax.random.fold_in(key, 7771), (KEY_VALUE_HEADS, HEAD_DIMENSION), 0, 2)
    return (random_bits * 2 - 1).astype(jnp.float32)


def draw_queries(key, part):
    own_key = jax.random.fold_in(key, 101)
    complete_shape = (REQUEST_COUNT, TREE_NODES, QUERY_HEADS * HEAD_DIMENSION)
    background = jnp.clip(2.0 * jax.random.normal(own_key, complete_shape, jnp.float32), -8.0, 8.0)
    value_pattern = sign_layout(key)
    spread_layout = jnp.repeat(value_pattern, QUERY_HEADS // KEY_VALUE_HEADS, axis=0).reshape(QUERY_HEADS * HEAD_DIMENSION)
    node_ids = jnp.arange(TREE_NODES)
    period = TREE_NODES // 4
    aligned = node_ids % period == TREE_NODES // 8
    strength = 5.6 + (node_ids // period % 3).astype(jnp.float32)
    inserted_entries = strength[:, None] * spread_layout[None, :]
    return jnp.where(aligned[None, :, None], inserted_entries[None], background).astype(jnp.bfloat16)


def draw_cache_keys(key, part):
    own_key = jax.random.fold_in(key, 202)
    complete_shape = (REQUEST_COUNT, KEY_VALUE_HEADS, CACHE_SLOTS, HEAD_DIMENSION)
    background = jnp.clip(jax.random.normal(own_key, complete_shape, jnp.float32), -4.5, 4.5)
    inserted_entries = 4.36 * sign_layout(key)[None, :, None, :]
    first_slot = (jnp.arange(CACHE_SLOTS) == 0)[None, None, :, None]
    return jnp.where(first_slot, inserted_entries, background).astype(jnp.bfloat16)


def draw_tree_keys(key, part):
    own_key = jax.random.fold_in(key, 303)
    complete_shape = (REQUEST_COUNT, TREE_NODES, KEY_VALUE_HEADS * HEAD_DIMENSION)
    background = jnp.clip(jax.random.normal(own_key, complete_shape, jnp.float32), -4.5, 4.5)
    inserted_entries = 4.4 * sign_layout(key).reshape(KEY_VALUE_HEADS * HEAD_DIMENSION)
    root_node = (jnp.arange(TREE_NODES) == 0)[None, :, None]
    return jnp.where(root_node, inserted_entries[None, None, :], background).astype(jnp.bfloat16)


def draw_parents(key, part):
    own_key = jax.random.fold_in(key, 404)
    draws = jax.random.randint(own_key, (REQUEST_COUNT, TREE_NODES), 0, 1 << 20)
    node_ids = jnp.arange(TREE_NODES, dtype=jnp.int32)
    chosen = draws % jnp.maximum(node_ids, 1)[None, :]
    return jnp.where(node_ids[None, :] == 0, 0, chosen).astype(jnp.int32)


def level_of(rng, extent, pieces, low, largest):
    factor_of, own = 1.0, jax.random.fold_in(rng, 6)
    for axis_at, parts in pieces:
        heights = jnp.exp(jax.random.uniform(jax.random.fold_in(own, axis_at), (parts,), jnp.float32, low / len(pieces), largest / len(pieces)))
        factor_of = factor_of * jnp.repeat(heights, extent[axis_at] // parts).reshape([-1 if axis == axis_at else 1 for axis in range(len(extent))])
    return factor_of


def profile(amount, total, reach, slope):
    portions = [(1 << 20) // math.isqrt(standing ** slope) + 1 for standing in range(2, amount + 1)]
    rest, given = total - reach - (amount - 1), [1] * (amount - 1)
    while rest > 0:
        candidates = [i for i in range(amount - 1) if given[i] < reach]
        mass, remaining = sum([portions[i] for i in candidates]), rest
        for i in candidates:
            more = min(reach - given[i], max(1, remaining * portions[i] // mass), rest)
            given[i] = given[i] + more
            rest = rest - more
    return np.array([reach] + given)


def uneven_parts(key, number_of, total, reach, skew):
    if number_of == 2:
        one = jax.random.randint(key, (), max(1, total - reach), min(reach, total - 1) + 1)
        return jnp.stack([one, total - one])
    tallies = jnp.asarray(profile(number_of, total, reach, skew), jnp.int32)
    couples = (number_of - 1) // 2
    giver, taker = tallies[1:1 + 2 * couples:2], tallies[2:2 + 2 * couples:2]
    slack = jnp.minimum(giver - 1, reach - taker)
    moved = jax.random.randint(jax.random.fold_in(key, 1), (couples,), 0, 1 << 20) % (slack + 1)
    tallies = tallies.at[1:1 + 2 * couples:2].set(giver - moved).at[2:2 + 2 * couples:2].set(taker + moved)
    return tallies[jax.random.permutation(jax.random.fold_in(key, 2), number_of)]


def noise(rng, extent, scale, most, shards=(), held_as=jnp.bfloat16):
    factor_of = level_of(rng, extent, shards, -0.22, 0.18) if shards else 1.0
    result = jax.random.normal(rng, extent, jnp.float32) * scale * factor_of
    return jnp.minimum(jnp.maximum(result, -most), most).astype(held_as)


def setup_inputs(seed: int = 0) -> dict:
    seeds = jax.random.split(jax.random.key(seed), 14)
    queries = draw_queries(jax.random.fold_in(seeds[13], 71), 0)
    tree_keys = draw_tree_keys(jax.random.fold_in(seeds[13], 71), 0)
    tree_token_values = noise(seeds[2], (REQUEST_COUNT, TREE_NODES, KEY_VALUE_HEADS * HEAD_DIMENSION), 1.0, 6.0, ((0, 8), (2, 2)))
    cache_keys = draw_cache_keys(jax.random.fold_in(seeds[13], 71), 0)
    cached_value_rows = noise(seeds[4], (REQUEST_COUNT, KEY_VALUE_HEADS, CACHE_SLOTS, HEAD_DIMENSION), 1.0, 6.0, ((0, 8), (1, 2), (2, 2)))
    lengths = uneven_parts(seeds[5], REQUEST_COUNT, REQUEST_COUNT * CACHE_SLOTS // 4, CACHE_SLOTS, 2).astype(jnp.int32)
    parents = draw_parents(jax.random.fold_in(seeds[13], 71), 0)
    residual = noise(seeds[7], (TOKENS, D), 1.0, 6.0, ((0, 16), (1, 2)), jnp.float32)
    out_weight = noise(seeds[8], (QUERY_HEADS * HEAD_DIMENSION, D), (QUERY_HEADS * HEAD_DIMENSION) ** -0.5, 0.0625, ((0, 2), (1, 16)))
    norm_gain = jnp.clip(1.0 + 0.15 * jax.random.normal(seeds[9], (D,), jnp.float32), 0.25, 1.75)
    gate_weight = noise(seeds[10], (D, FF), D ** -0.5, 0.0625, ((0, 2), (1, 16)))
    up_weight = noise(seeds[11], (D, FF), D ** -0.5, 0.0625, ((0, 2), (1, 16)))
    down_weight = noise(seeds[12], (FF, D), FF ** -0.5, 0.03125, ((0, 16), (1, 2)))
    return dict(queries=queries, tree_keys=tree_keys, tree_token_values=tree_token_values, cache_keys=cache_keys, cached_value_rows=cached_value_rows, lengths=lengths, parents=parents, residual=residual, out_weight=out_weight, norm_gain=norm_gain, gate_weight=gate_weight, up_weight=up_weight, down_weight=down_weight)


MASKED = -1e+30
EPSILON = 1e-05

def ancestors(parent_row, node_total):
    node_ids = jnp.arange(node_total, dtype=jnp.int32)
    upward = (parent_row[:, None] == node_ids[None, :]).astype(jnp.float32)
    reachable = jnp.minimum(jnp.eye(node_total, dtype=jnp.float32) + upward, 1.0)
    for repeat_count in range((node_total - 1).bit_length()):
        reachable = jnp.minimum(jnp.dot(reachable, reachable, precision=lax.Precision.HIGHEST), 1.0)
    return reachable > 0.5

def attend_request(inputs):
    query_tile_rows, tree_key_rows, tree_value_block, keys_all, values_all, length, parent_row = inputs
    query_group_width = QUERY_HEADS // KEY_VALUE_HEADS
    score_scale = HEAD_DIMENSION ** (-0.5)
    query_complete = query_tile_rows.astype(jnp.float32).reshape(TREE_NODES, KEY_VALUE_HEADS, query_group_width, HEAD_DIMENSION)
    cache_scores = jnp.einsum('nhgd,hpd->hgnp', query_complete, keys_all.astype(jnp.float32)) * score_scale
    tree_complete = tree_key_rows.astype(jnp.float32).reshape(TREE_NODES, KEY_VALUE_HEADS, HEAD_DIMENSION)
    tree_score_matrix = jnp.einsum('czpk,izk->zpci', query_complete, tree_complete) * score_scale
    positions = jnp.arange(CACHE_SLOTS, dtype=jnp.int32)
    cache_usable = jnp.broadcast_to((positions < length)[None, None, None, :], cache_scores.shape)
    tree_usable = jnp.broadcast_to(ancestors(parent_row, TREE_NODES)[None, None], tree_score_matrix.shape)
    scores = jnp.concatenate([cache_scores, tree_score_matrix], axis=-1)
    usable = jnp.concatenate([cache_usable, tree_usable], axis=-1)
    scores = jnp.where(usable, scores, MASKED)
    highest = lax.optimization_barrier(jnp.max(scores, axis=-1, keepdims=True))
    weights = jnp.where(usable, jnp.exp(scores - highest), 0.0)
    total = lax.optimization_barrier(jnp.sum(weights, axis=-1))
    tree_value_rows = tree_value_block.astype(jnp.float32).reshape(TREE_NODES, KEY_VALUE_HEADS, HEAD_DIMENSION).transpose(1, 0, 2)
    values = jnp.concatenate([values_all.astype(jnp.float32), tree_value_rows], axis=1)
    mixed = jnp.einsum('hgnk,hkd->hgnd', weights, values, precision=lax.Precision.HIGHEST) / total[..., None]
    return mixed.transpose(2, 0, 1, 3).reshape(TREE_NODES, QUERY_HEADS * HEAD_DIMENSION).astype(jnp.bfloat16)

def reference(queries, tree_keys, tree_token_values, cache_keys, cached_value_rows, lengths, parents, residual, out_weight, norm_gain, gate_weight, up_weight, down_weight):
    attention = lax.map(attend_request, (queries, tree_keys, tree_token_values, cache_keys, cached_value_rows, lengths, parents))
    attention = attention.reshape(TOKENS, QUERY_HEADS * HEAD_DIMENSION)
    state = residual + jnp.dot(attention, out_weight, preferred_element_type=jnp.float32)
    mean_square = lax.optimization_barrier(jnp.mean(state * state, axis=1, keepdims=True))
    normed = (state * lax.rsqrt(mean_square + EPSILON) * norm_gain).astype(jnp.bfloat16)
    gate = jnp.dot(normed, gate_weight, preferred_element_type=jnp.float32)
    upward = jnp.dot(normed, up_weight, preferred_element_type=jnp.float32)
    activation = (jax.nn.silu(gate) * upward).astype(jnp.bfloat16)
    return state + jnp.dot(activation, down_weight, preferred_element_type=jnp.float32)
```

```python
import functools
import math

import jax
import jax.numpy as jnp
from jax import lax
from jax.experimental import pallas as pl
from jax.experimental.pallas import tpu as pltpu
from jax.sharding import PartitionSpec as P

MASKED = -1e30
EPSILON = 1e-05


def attend(len_ref, q_ref, tk_ref, tv_ref, k_ref, v_ref, par_ref, o_ref, ml_ref, acc, stat, *, chunk, factor):
    live = len_ref[0]
    tree_live = len_ref[1]
    nodes = q_ref.shape[0]
    size = k_ref.shape[-1]
    group = q_ref.shape[1] // size
    rows = nodes * group
    q = jnp.concatenate([q_ref[:, g * size : (g + 1) * size] for g in range(group)], axis=0)
    acc[...] = jnp.zeros_like(acc)
    stat[0:1, :] = jnp.full((1, rows), MASKED, jnp.float32)
    stat[1:2, :] = jnp.zeros((1, rows), jnp.float32)

    def scores_of(keys):
        return lax.dot_general(keys, q, (((1,), (1,)), ((), ())), preferred_element_type=jnp.float32)

    def absorb(scores, usable, values):
        if usable is not None:
            scores = jnp.where(usable, scores, MASKED)
        old = stat[0:1, :]
        top = jnp.maximum(old, jnp.max(scores, axis=0, keepdims=True))
        weights = jnp.exp2(scores * factor - top * factor)
        if usable is not None:
            weights = jnp.where(usable, weights, 0.0)
        shrink = jnp.exp2((old - top) * factor)
        stat[0:1, :] = top
        stat[1:2, :] = stat[1:2, :] * shrink + jnp.sum(weights, axis=0, keepdims=True)
        acc[...] = acc[...] * shrink + lax.dot_general(
            values, weights.astype(jnp.bfloat16), (((0,), (0,)), ((), ())), preferred_element_type=jnp.float32
        )

    full = live // chunk

    def visit(c, carry):
        at = pl.ds(pl.multiple_of(c * chunk, chunk), chunk)
        absorb(scores_of(k_ref[0, at, :]), None, v_ref[0, at, :])
        return carry

    lax.fori_loop(0, full, visit, 0)

    @pl.when(live > full * chunk)
    def _():
        at = pl.ds(pl.multiple_of(full * chunk, chunk), chunk)
        spot = full * chunk + lax.broadcasted_iota(jnp.int32, (chunk, rows), 0)
        absorb(scores_of(k_ref[0, at, :]), spot < live, v_ref[0, at, :])

    @pl.when(tree_live > 0)
    def _():
        up = lax.broadcasted_iota(jnp.int32, (nodes, nodes), 0)
        across = lax.broadcasted_iota(jnp.int32, (nodes, nodes), 1)
        link = jnp.where(up == par_ref[...], 1.0, 0.0) + jnp.where(up == across, 1.0, 0.0)
        reach = jnp.minimum(link, 1.0)
        for _ in range((nodes - 1).bit_length()):
            half = reach.astype(jnp.bfloat16)
            reach = jnp.minimum(jnp.dot(half, half, preferred_element_type=jnp.float32), 1.0)
        row = lax.broadcasted_iota(jnp.int32, (nodes, rows), 0)
        col = lax.broadcasted_iota(jnp.int32, (nodes, rows), 1)
        spread = jnp.where(lax.rem(col, nodes) == row, 1.0, 0.0).astype(jnp.bfloat16)
        mask = jnp.dot(reach.astype(jnp.bfloat16), spread, preferred_element_type=jnp.float32)
        absorb(scores_of(tk_ref[...]), mask > 0.5, tv_ref[...])

    total = stat[1:2, :]
    out = (acc[...] / jnp.where(total > 0.0, total, 1.0)).T.astype(jnp.bfloat16)
    for g in range(group):
        o_ref[:, g * size : (g + 1) * size] = out[g * nodes : (g + 1) * nodes, :]
    ml_ref[0] = jnp.concatenate([stat[0:1, :] * (size**-0.5), total], axis=0)


def attention_part(queries, tree_keys, tree_values, keys, values, lengths2, parents):
    heads, span, size = keys.shape
    nodes, width = queries.shape
    wide = width // heads
    rows = wide // size * nodes
    chunk = math.gcd(span, 1024)
    body = functools.partial(attend, chunk=chunk, factor=size**-0.5 * math.log2(math.e))
    return pl.pallas_call(
        body,
        out_shape=(
            jax.ShapeDtypeStruct((nodes, width), jnp.bfloat16),
            jax.ShapeDtypeStruct((heads, 2, rows), jnp.float32),
        ),
        grid_spec=pltpu.PrefetchScalarGridSpec(
            num_scalar_prefetch=1,
            grid=(heads,),
            in_specs=[
                pl.BlockSpec((nodes, wide), lambda h, n: (0, h)),
                pl.BlockSpec((nodes, size), lambda h, n: (0, h)),
                pl.BlockSpec((nodes, size), lambda h, n: (0, h)),
                pl.BlockSpec((1, span, size), lambda h, n: (h, 0, 0)),
                pl.BlockSpec((1, span, size), lambda h, n: (h, 0, 0)),
                pl.BlockSpec((1, nodes), lambda h, n: (0, 0)),
            ],
            out_specs=(
                pl.BlockSpec((nodes, wide), lambda h, n: (0, h)),
                pl.BlockSpec((1, 2, rows), lambda h, n: (h, 0, 0)),
            ),
            scratch_shapes=[
                pltpu.VMEM((size, rows), jnp.float32),
                pltpu.VMEM((8, rows), jnp.float32),
            ],
        ),
        compiler_params=pltpu.CompilerParams(dimension_semantics=("arbitrary",)),
    )(lengths2, queries, tree_keys, tree_values, keys, values, parents)


MESH = pl.DeviceIdType.MESH
VMEM_LIMIT = 60 * 1024 * 1024


def split_count(n):
    lo = math.isqrt(n)
    while n % lo:
        lo -= 1
    return n // lo, lo


def ring_peers(n, me):
    return [lax.rem(me + d, n) for d in range(1, n)]


def staged_places(hi_n, lo_n, core_n):
    req = lax.axis_index("req")
    hi, lo, core = req // lo_n, lax.rem(req, lo_n), lax.axis_index("ffn")
    hi_peers = [(h, {"req": h * lo_n + lo}) for h in ring_peers(hi_n, hi)]
    lo_peers = [(b, {"req": hi * lo_n + b}) for b in ring_peers(lo_n, lo)]
    core_peers = [(c, {"ffn": c}) for c in ring_peers(core_n, core)]
    return hi, lo, core, hi_peers, lo_peers, core_peers


def meet(peers):
    barrier = pltpu.get_barrier_semaphore()
    for _, where in peers:
        pl.semaphore_signal(barrier, inc=1, device_id=where, device_id_type=MESH)
    pl.semaphore_wait(barrier, len(peers))


def remote(src, dst, send, recv, where):
    return pltpu.make_async_remote_copy(
        src_ref=src, dst_ref=dst, send_sem=send, recv_sem=recv, device_id=where, device_id_type=MESH
    )


def gather_body(x_ref, out_ref, send, recv, own_sem, *, dims, pieces):
    hi_n, lo_n, core_n = dims
    hi, lo, core, hi_peers, lo_peers, core_peers = staged_places(*dims)
    wide = x_ref.shape[1] // pieces
    meet(hi_peers + lo_peers + core_peers)
    own = pltpu.make_async_copy(x_ref, out_ref.at[hi, lo, core], own_sem)
    own.start()
    first, second, third = [], [], []
    for p in range(pieces):
        cols = pl.ds(p * wide, wide)
        group = []
        for d, (_, where) in enumerate(hi_peers):
            copy = remote(
                x_ref.at[:, cols], out_ref.at[hi, lo, core, :, cols], send.at[p, d], recv.at[p, d], where
            )
            copy.start()
            group.append(copy)
        first.append(group)
    own.wait()
    base = len(hi_peers)
    for step in range(pieces + 1):
        if step < pieces:
            cols = pl.ds(step * wide, wide)
            for copy in first[step]:
                copy.wait_recv()
            group = []
            for d, (_, where) in enumerate(lo_peers):
                part = out_ref.at[:, lo, core, :, cols]
                copy = remote(part, part, send.at[step, base + d], recv.at[step, base + d], where)
                copy.start()
                group.append(copy)
            second.append(group)
        if step > 0:
            p = step - 1
            cols = pl.ds(p * wide, wide)
            for copy in second[p]:
                copy.wait_recv()
            group = []
            for d, (_, where) in enumerate(core_peers):
                at = base + len(lo_peers) + d
                part = out_ref.at[:, :, core, :, cols]
                copy = remote(part, part, send.at[p, at], recv.at[p, at], where)
                copy.start()
                group.append(copy)
            third.append(group)
    for group in third:
        for copy in group:
            copy.wait_recv()
    for group in first + second + third:
        for copy in group:
            copy.wait_send()


def gather_tokens(x, collective_id):
    dims = (*split_count(lax.axis_size("req")), lax.axis_size("ffn"))
    rows, width = x.shape
    pieces = math.gcd(width // 128, 4)
    links = sum(dims) - 3
    vmem = pl.BlockSpec(memory_space=pltpu.VMEM)
    out = pl.pallas_call(
        functools.partial(gather_body, dims=dims, pieces=pieces),
        out_shape=jax.ShapeDtypeStruct((*dims, rows, width), x.dtype),
        in_specs=[vmem],
        out_specs=vmem,
        scratch_shapes=[
            pltpu.SemaphoreType.DMA((pieces, links)),
            pltpu.SemaphoreType.DMA((pieces, links)),
            pltpu.SemaphoreType.DMA,
        ],
        compiler_params=pltpu.CompilerParams(
            collective_id=collective_id, has_side_effects=True, vmem_limit_bytes=VMEM_LIMIT
        ),
    )(x)
    return out.reshape(math.prod(dims) * rows, width)


def lane_block(width, most):
    return max(b for b in range(128, most + 1, 128) if width % b == 0)


def ffn_body(
    x_ref, state_ref, gate_hbm, up_hbm, down_hbm, out_ref,
    gath, wgu, wd, rbuf, part, got, act, dbuf, got_core, mid, own_mid, got_lo, low, own_low, got_hi,
    own_sem, w_sem, wd_sem, g_send, g_recv, p_send, p_recv, a_send, a_recv, c_send, c_recv, l_send, l_recv, h_send, h_recv,
    *, dims, kn, rc,
):
    hn, ln, cn = dims
    hi, lo, core, _, _, _ = staged_places(*dims)
    k = lax.axis_index("kvh")
    chunks = x_ref.shape[0] // rc
    blocks = hn * ln
    hc = wgu.shape[2] // 2
    hs = wgu.shape[0]
    total_rows = blocks * cn * rc
    keep = total_rows // kn
    fw = wd.shape[2]
    fs = x_ref.shape[1] // fw
    wd_slots, d_slots, r_slots, m_slots = wd.shape[0], dbuf.shape[0], rbuf.shape[0], own_mid.shape[0]
    to_hi = lambda d: (lax.rem(hi + d, hn), {"req": lax.rem(hi + d, hn) * ln + lo})
    to_lo = lambda d: (lax.rem(lo + d, ln), {"req": hi * ln + lax.rem(lo + d, ln)})
    to_core = lambda d: (lax.rem(core + d, cn), {"ffn": lax.rem(core + d, cn)})
    to_kvh = lambda d: (lax.rem(k + d, kn), {"kvh": lax.rem(k + d, kn)})
    meet(
        [to_hi(d) for d in range(1, hn)]
        + [to_lo(d) for d in range(1, ln)]
        + [to_core(d) for d in range(1, cn)]
        + [to_kvh(d) for d in range(1, kn)]
    )

    def weight_copies(h):
        cols = pl.ds(pl.multiple_of(h * hc, hc), hc)
        return (
            pltpu.make_async_copy(gate_hbm.at[:, cols], wgu.at[h, :, pl.ds(0, hc)], w_sem.at[0, h]),
            pltpu.make_async_copy(up_hbm.at[:, cols], wgu.at[h, :, pl.ds(hc, hc)], w_sem.at[1, h]),
        )

    def down_copy(j):
        slot = lax.rem(j, wd_slots)
        cols = pl.ds(pl.multiple_of(lax.rem(j, fs) * fw, fw), fw)
        return pltpu.make_async_copy(down_hbm.at[:, cols], wd.at[slot], wd_sem.at[slot])

    def rows_of(h, b, c):
        return pl.ds(pl.multiple_of(((c * ln + b) * hn + h) * rc, rc), rc)

    def place(c, e, g, f):
        return gath.at[c, rows_of(lax.rem(hi + hn - e, hn), lax.rem(lo + ln - g, ln), f), :]

    base_lo = hn - 1
    base_core = base_lo + hn * (ln - 1)

    def hi_copy(c, d):
        at = d - 1
        src = x_ref.at[pl.ds(c * rc, rc), :]
        return remote(src, place(c, 0, 0, core), g_send.at[c, at], g_recv.at[c, at], to_hi(d)[1])

    def lo_copy(c, e, d):
        at = base_lo + e * (ln - 1) + d - 1
        src = x_ref.at[pl.ds(c * rc, rc), :] if e == 0 else place(c, e, 0, core)
        return remote(src, place(c, e, 0, core), g_send.at[c, at], g_recv.at[c, at], to_lo(d)[1])

    def core_copy(c, e, g, d):
        at = base_core + (e * ln + g) * (cn - 1) + d - 1
        src = x_ref.at[pl.ds(c * rc, rc), :] if e == 0 and g == 0 else place(c, e, g, core)
        return remote(src, place(c, e, g, core), g_send.at[c, at], g_recv.at[c, at], to_core(d)[1])

    hi_order = sorted(range(1, hn), key=lambda d: min(d, hn - d))

    def own_copy(c):
        return pltpu.make_async_copy(x_ref.at[pl.ds(c * rc, rc), :], place(c, 0, 0, core), own_sem.at[c])

    def gather_start(c):
        for d in hi_order:
            hi_copy(c, d).start()
        for d in range(1, ln):
            lo_copy(c, 0, d).start()
        for d in range(1, cn):
            core_copy(c, 0, 0, d).start()
        own_copy(c).start()

    def gather_hi(c):
        for e in hi_order:
            hi_copy(c, e).wait_recv()
            for d in range(1, ln):
                lo_copy(c, e, d).start()
            for d in range(1, cn):
                core_copy(c, e, 0, d).start()

    def gather_lo(c):
        for e in [0] + hi_order:
            for g in range(1, ln):
                lo_copy(c, e, g).wait_recv()
                for d in range(1, cn):
                    core_copy(c, e, g, d).start()

    def gather_end(c):
        for e in [0] + hi_order:
            for g in range(ln):
                for d in range(1, cn):
                    core_copy(c, e, g, d).wait_recv()
        own_copy(c).wait()

    def gather_sent(c):
        for d in range(1, hn):
            hi_copy(c, d).wait_send()
        for e in range(hn):
            for d in range(1, ln):
                lo_copy(c, e, d).wait_send()
            for g in range(ln):
                for d in range(1, cn):
                    core_copy(c, e, g, d).wait_send()

    def part_copy(s, d):
        return remote(part.at[s, d - 1], got.at[s, d - 1], p_send.at[s, d - 1], p_recv.at[s, d - 1], to_kvh(d)[1])

    def hidden(c, h):
        s = c * hs + h
        slot = lax.rem(s, r_slots)
        rbuf[slot] = jnp.dot(gath[c], wgu[h], preferred_element_type=jnp.float32)
        for d in range(1, kn):
            group = pl.ds(pl.multiple_of(to_kvh(d)[0] * keep, keep), keep)
            part[s, d - 1] = rbuf[slot, group, :].astype(jnp.bfloat16)
            part_copy(s, d).start()

    mine = pl.ds(pl.multiple_of(k * keep, keep), keep)

    def act_copy(s, d):
        c, h = lax.div(s, hs), lax.rem(s, hs)
        spot = act.at[c, mine, pl.ds(pl.multiple_of(h * hc, hc), hc)]
        return remote(spot, spot, a_send.at[s, d - 1], a_recv.at[s, d - 1], to_kvh(d)[1])

    def activate(s):
        c, h = lax.div(s, hs), lax.rem(s, hs)
        slot = lax.rem(s, r_slots)
        for d in range(1, kn):
            part_copy(s, d).wait_recv()
        gate = rbuf[slot, mine, pl.ds(0, hc)]
        up = rbuf[slot, mine, pl.ds(hc, hc)]
        for d in range(kn - 1):
            gate = gate + got[s, d, :, pl.ds(0, hc)].astype(jnp.float32)
            up = up + got[s, d, :, pl.ds(hc, hc)].astype(jnp.float32)
        act[c, mine, pl.ds(pl.multiple_of(h * hc, hc), hc)] = (gate / (1.0 + jnp.exp(-gate)) * up).astype(jnp.bfloat16)
        for d in range(1, kn):
            act_copy(s, d).start()

    def activated(c):
        def one(h, carry):
            for d in range(1, kn):
                act_copy(c * hs + h, d).wait_recv()
            return carry

        lax.fori_loop(0, hs, one, 0)

    def down_send(j, d):
        half = pl.ds(pl.multiple_of(to_core(d)[0] * (blocks * rc), blocks * rc), blocks * rc)
        return remote(
            dbuf.at[lax.rem(j, d_slots), half, :], got_core.at[j, d - 1], c_send.at[j, d - 1], c_recv.at[j, d - 1], to_core(d)[1]
        )

    def mid_send(j, d):
        return remote(mid.at[j, d - 1], got_lo.at[j, d - 1], l_send.at[j, d - 1], l_recv.at[j, d - 1], to_lo(d)[1])

    def low_send(j, d):
        return remote(low.at[j, d - 1], got_hi.at[j, d - 1], h_send.at[j, d - 1], h_recv.at[j, d - 1], to_hi(d)[1])

    def down(j):
        c = lax.div(j, fs)
        slot = lax.rem(j, d_slots)

        @pl.when(j >= d_slots)
        def _():
            for d in range(1, cn):
                down_send(j - d_slots, d).wait_send()

        down_copy(j).wait()
        dbuf[slot] = jnp.dot(act[c], wd[lax.rem(j, wd_slots)], preferred_element_type=jnp.float32)

        @pl.when(j + wd_slots < chunks * fs)
        def _():
            down_copy(j + wd_slots).start()

        for d in range(1, cn):
            down_send(j, d).start()

    def add_core(j):
        slot = lax.rem(j, d_slots)
        for d in range(1, cn):
            down_send(j, d).wait_recv()

        def total(b):
            at = pl.multiple_of(b * (hn * rc), hn * rc)
            here = pl.multiple_of(core * (blocks * rc), blocks * rc) + at
            result = dbuf[slot, pl.ds(pl.multiple_of(here, hn * rc), hn * rc), :]
            for d in range(cn - 1):
                result = result + got_core[j, d, pl.ds(at, hn * rc), :]
            return result

        for d in range(1, ln):
            mid[j, d - 1] = total(to_lo(d)[0]).astype(jnp.bfloat16)
            mid_send(j, d).start()
        own_mid[lax.rem(j, m_slots)] = total(lo)

    def add_lo(j):
        slot = lax.rem(j, m_slots)
        for d in range(1, ln):
            mid_send(j, d).wait_recv()

        def total(h):
            at = pl.ds(pl.multiple_of(h * rc, rc), rc)
            result = own_mid[slot, at, :]
            for d in range(ln - 1):
                result = result + got_lo[j, d, at, :].astype(jnp.float32)
            return result

        for d in range(1, hn):
            low[j, d - 1] = total(to_hi(d)[0]).astype(jnp.bfloat16)
            low_send(j, d).start()
        own_low[slot] = total(hi)

    def add_hi(j):
        c, n = lax.div(j, fs), lax.rem(j, fs)
        for d in range(1, hn):
            low_send(j, d).wait_recv()
        result = own_low[lax.rem(j, m_slots)]
        for d in range(hn - 1):
            result = result + got_hi[j, d].astype(jnp.float32)
        at = (pl.ds(pl.multiple_of(c * rc, rc), rc), pl.ds(pl.multiple_of(n * fw, fw), fw))
        out_ref[at] = state_ref[at] + result

    pieces = chunks * fs
    lag = 2

    def piece(j):
        for depth, stage in enumerate((down, add_core, add_lo, add_hi)):

            @pl.when((j >= depth * lag) & (j < pieces + depth * lag))
            def _(depth=depth, stage=stage):
                stage(j - depth * lag)

    for h in range(hs):
        for copy in weight_copies(h):
            copy.start()
    for j in range(min(wd_slots, pieces)):
        down_copy(j).start()
    gather_start(0)
    gather_hi(0)
    gather_lo(0)
    for c in range(1, chunks):
        gather_start(c)
    gather_end(0)
    behind = 2
    marks = {3: gather_hi, 5: gather_lo, hs - 1: gather_end}
    per = -(-fs // (hs - 3))
    for c in range(chunks):

        def step(h, carry, c=c):
            if c == 0:
                for copy in weight_copies(h):
                    copy.wait()
            hidden(c, h)

            @pl.when(c * hs + h >= behind)
            def _():
                activate(c * hs + h - behind)

            if c + 1 < chunks:
                for at, stage in marks.items():

                    @pl.when(h == at)
                    def _(stage=stage):
                        stage(c + 1)

            if c > 0:

                @pl.when(h == 3)
                def _():
                    activated(c - 1)

                @pl.when(h >= 3)
                def _():
                    def one(i, carry):
                        piece((c - 1) * fs + (h - 3) * per + i)
                        return carry

                    lax.fori_loop(0, jnp.minimum(per, fs - (h - 3) * per), one, 0)

            return carry

        lax.fori_loop(0, hs, step, 0)
    for s in range(chunks * hs - behind, chunks * hs):
        activate(s)
    activated(chunks - 1)

    def last(j, carry):
        piece(j)
        return carry

    lax.fori_loop((chunks - 1) * fs, pieces + 3 * lag, last, 0)
    for c in range(chunks):
        gather_sent(c)

    def sent_steps(s, carry):
        for d in range(1, kn):
            part_copy(s, d).wait_send()
            act_copy(s, d).wait_send()
        return carry

    lax.fori_loop(0, chunks * hs, sent_steps, 0)

    def sent_pieces(j, carry):
        @pl.when(j >= pieces - d_slots)
        def _():
            for d in range(1, cn):
                down_send(j, d).wait_send()

        for d in range(1, ln):
            mid_send(j, d).wait_send()
        for d in range(1, hn):
            low_send(j, d).wait_send()
        return carry

    lax.fori_loop(0, pieces, sent_pieces, 0)


def feed_forward(x, state, gate_weight, up_weight, down_weight, collective_id):
    hn, ln = split_count(lax.axis_size("req"))
    cn, kn = lax.axis_size("ffn"), lax.axis_size("kvh")
    rows, width = x.shape
    rc = math.gcd(rows, 16)
    chunks = rows // rc
    hidden = gate_weight.shape[1]
    hc = lane_block(hidden, 256)
    hs = hidden // hc
    fw = lane_block(width, max(128, width // 8))
    pieces = chunks * (width // fw)
    tokens = hn * ln * cn * rc
    keep = tokens // kn
    links = (hn - 1) + hn * (ln - 1) + hn * ln * (cn - 1)
    vmem = pl.BlockSpec(memory_space=pltpu.VMEM)
    hbm = pl.BlockSpec(memory_space=pl.ANY)
    f32, b16 = jnp.float32, jnp.bfloat16
    dma = pltpu.SemaphoreType.DMA
    steps = chunks * hs
    return pl.pallas_call(
        functools.partial(ffn_body, dims=(hn, ln, cn), kn=kn, rc=rc),
        out_shape=jax.ShapeDtypeStruct(state.shape, f32),
        in_specs=[vmem, vmem, hbm, hbm, hbm],
        out_specs=vmem,
        scratch_shapes=[
            pltpu.VMEM((chunks, tokens, width), b16),
            pltpu.VMEM((hs, width, 2 * hc), b16),
            pltpu.VMEM((3, hidden, fw), b16),
            pltpu.VMEM((3, tokens, 2 * hc), f32),
            pltpu.VMEM((steps, kn - 1, keep, 2 * hc), b16),
            pltpu.VMEM((steps, kn - 1, keep, 2 * hc), b16),
            pltpu.VMEM((chunks, tokens, hidden), b16),
            pltpu.VMEM((4, tokens, fw), f32),
            pltpu.VMEM((pieces, cn - 1, hn * ln * rc, fw), f32),
            pltpu.VMEM((pieces, ln - 1, hn * rc, fw), b16),
            pltpu.VMEM((4, hn * rc, fw), f32),
            pltpu.VMEM((pieces, ln - 1, hn * rc, fw), b16),
            pltpu.VMEM((pieces, hn - 1, rc, fw), b16),
            pltpu.VMEM((4, rc, fw), f32),
            pltpu.VMEM((pieces, hn - 1, rc, fw), b16),
            dma((chunks,)),
            dma((2, hs)),
            dma((3,)),
            dma((chunks, links)),
            dma((chunks, links)),
            dma((steps, kn - 1)),
            dma((steps, kn - 1)),
            dma((steps, kn - 1)),
            dma((steps, kn - 1)),
            dma((pieces, cn - 1)),
            dma((pieces, cn - 1)),
            dma((pieces, ln - 1)),
            dma((pieces, ln - 1)),
            dma((pieces, hn - 1)),
            dma((pieces, hn - 1)),
        ],
        compiler_params=pltpu.CompilerParams(
            collective_id=collective_id, has_side_effects=True, vmem_limit_bytes=63 * 1024 * 1024
        ),
    )(x, state, gate_weight, up_weight, down_weight)


def local(
    queries,
    tree_keys,
    tree_token_values,
    cache_keys,
    cached_value_rows,
    lengths,
    parents,
    residual,
    out_weight,
    norm_gain,
    gate_weight,
    up_weight,
    down_weight,
):
    heads, half_len, size = cache_keys.shape[1:]
    nodes = queries.shape[1]
    group = queries.shape[2] // (heads * size)
    request_index = lax.axis_index("req")
    half_index = lax.axis_index("ffn")
    halves = lax.axis_size("ffn")
    features = norm_gain.shape[0] * lax.axis_size("kvh")
    length = lax.dynamic_index_in_dim(lengths, request_index, keepdims=False)
    live_len = jnp.clip(length - half_index * half_len, 0, half_len)
    lengths2 = jnp.stack([live_len, (half_index == 0).astype(jnp.int32)])
    own, ml = attention_part(
        queries[0], tree_keys[0], tree_token_values[0], cache_keys[0], cached_value_rows[0], lengths2, parents
    )
    mine_rows = nodes // halves
    pair = lax.all_to_all(own, "ffn", split_axis=0, concat_axis=0, tiled=True).reshape(halves, mine_rows, -1)
    ml_pair = lax.all_gather(ml, "ffn")
    weights = ml_pair[:, :, 1] * jnp.exp(ml_pair[:, :, 0] - jnp.max(ml_pair[:, :, 0], axis=0))
    share = (weights / jnp.sum(weights, axis=0)).reshape(halves, heads * group, nodes)
    share = lax.dynamic_slice_in_dim(share, half_index * mine_rows, mine_rows, 2).transpose(0, 2, 1)[..., None]
    mixed = jnp.sum(pair.astype(jnp.float32).reshape(halves, mine_rows, heads * group, size) * share, axis=0)
    attention = mixed.astype(jnp.bfloat16).reshape(mine_rows, heads * group * size)
    partial_rows = jnp.dot(gather_tokens(attention, 1), out_weight, preferred_element_type=jnp.float32)
    regrouped = lax.all_to_all(
        partial_rows.astype(jnp.bfloat16), ("req", "ffn"), split_axis=0, concat_axis=1, tiled=True
    )
    shares = lax.all_to_all(regrouped, "kvh", split_axis=1, concat_axis=0, tiled=True)
    projected = jnp.sum(shares.astype(jnp.float32).reshape(-1, *residual.shape), axis=0)
    state = residual + projected
    squares = lax.psum(jnp.sum(state * state, axis=1), "kvh")
    normed = (state * lax.rsqrt(squares / features + EPSILON)[:, None] * norm_gain).astype(jnp.bfloat16)
    return feed_forward(normed, state, gate_weight, up_weight, down_weight, 2)


def solution(mesh):
    in_specs = (
        P("req", None, "kvh"),
        P("req", None, "kvh"),
        P("req", None, "kvh"),
        P("req", "kvh", "ffn", None),
        P("req", "kvh", "ffn", None),
        P(),
        P("req", None),
        P(("req", "ffn"), "kvh"),
        P("kvh", ("req", "ffn")),
        P("kvh"),
        P("kvh", ("req", "ffn")),
        P("kvh", ("req", "ffn")),
        P(("req", "ffn"), "kvh"),
    )
    out_specs = P(("req", "ffn"), "kvh")
    return jax.shard_map(local, mesh=mesh, in_specs=in_specs, out_specs=out_specs, check_vma=False)
```

```python
import functools
import math

import jax
import jax.numpy as jnp
from jax import lax
from jax.experimental import pallas as pl
from jax.experimental.pallas import tpu as pltpu
from jax.sharding import PartitionSpec as P

MASKED = -1e30
EPSILON = 1e-05


MESH = pl.DeviceIdType.MESH
VMEM_LIMIT = 60 * 1024 * 1024


def split_count(n):
    lo = math.isqrt(n)
    while n % lo:
        lo -= 1
    return n // lo, lo


def ring_peers(n, me):
    return [lax.rem(me + d, n) for d in range(1, n)]


def staged_places(hi_n, lo_n, core_n):
    req = lax.axis_index("req")
    hi, lo, core = req // lo_n, lax.rem(req, lo_n), lax.axis_index("ffn")
    hi_peers = [(h, {"req": h * lo_n + lo}) for h in ring_peers(hi_n, hi)]
    lo_peers = [(b, {"req": hi * lo_n + b}) for b in ring_peers(lo_n, lo)]
    core_peers = [(c, {"ffn": c}) for c in ring_peers(core_n, core)]
    return hi, lo, core, hi_peers, lo_peers, core_peers


def meet(peers):
    barrier = pltpu.get_barrier_semaphore()
    for _, where in peers:
        pl.semaphore_signal(barrier, inc=1, device_id=where, device_id_type=MESH)
    pl.semaphore_wait(barrier, len(peers))


def remote(src, dst, send, recv, where):
    return pltpu.make_async_remote_copy(
        src_ref=src, dst_ref=dst, send_sem=send, recv_sem=recv, device_id=where, device_id_type=MESH
    )


def token_gather(dims, rc, source, target, send, recv, own_sem):
    hn, ln, cn = dims
    req = lax.axis_index("req")
    hi, lo, core = req // ln, lax.rem(req, ln), lax.axis_index("ffn")
    to_hi = lambda d: {"req": lax.rem(hi + d, hn) * ln + lo}
    to_lo = lambda d: {"req": hi * ln + lax.rem(lo + d, ln)}
    to_core = lambda d: {"ffn": lax.rem(core + d, cn)}
    hi_order = sorted(range(1, hn), key=lambda d: min(d, hn - d))
    base_lo = hn - 1
    base_core = base_lo + hn * (ln - 1)

    def place(c, e, g):
        b = (core * ln + lax.rem(lo + ln - g, ln)) * hn + lax.rem(hi + hn - e, hn)
        return target(c, pl.ds(pl.multiple_of(b * rc, rc), rc))

    def hi_copy(c, d):
        at = d - 1
        return remote(source(c), place(c, 0, 0), send.at[c, at], recv.at[c, at], to_hi(d))

    def lo_copy(c, e, d):
        at = base_lo + e * (ln - 1) + d - 1
        src = source(c) if e == 0 else place(c, e, 0)
        return remote(src, place(c, e, 0), send.at[c, at], recv.at[c, at], to_lo(d))

    def core_copy(c, e, g, d):
        at = base_core + (e * ln + g) * (cn - 1) + d - 1
        src = source(c) if e == 0 and g == 0 else place(c, e, g)
        return remote(src, place(c, e, g), send.at[c, at], recv.at[c, at], to_core(d))

    def own_copy(c):
        return pltpu.make_async_copy(source(c), place(c, 0, 0), own_sem.at[c])

    def start(c):
        for d in hi_order:
            hi_copy(c, d).start()
        for d in range(1, ln):
            lo_copy(c, 0, d).start()
        for d in range(1, cn):
            core_copy(c, 0, 0, d).start()
        own_copy(c).start()

    def pass_hi(c):
        for e in hi_order:
            hi_copy(c, e).wait_recv()
            for d in range(1, ln):
                lo_copy(c, e, d).start()
            for d in range(1, cn):
                core_copy(c, e, 0, d).start()

    def pass_lo(c):
        for e in [0] + hi_order:
            for g in range(1, ln):
                lo_copy(c, e, g).wait_recv()
                for d in range(1, cn):
                    core_copy(c, e, g, d).start()

    def finish(c):
        for e in [0] + hi_order:
            for g in range(ln):
                for d in range(1, cn):
                    core_copy(c, e, g, d).wait_recv()
        own_copy(c).wait()

    def sent(c):
        for d in range(1, hn):
            hi_copy(c, d).wait_send()
        for e in range(hn):
            for d in range(1, ln):
                lo_copy(c, e, d).wait_send()
            for g in range(ln):
                for d in range(1, cn):
                    core_copy(c, e, g, d).wait_send()

    return start, pass_hi, pass_lo, finish, sent


def gather_links(dims):
    hn, ln, cn = dims
    return (hn - 1) + hn * (ln - 1) + hn * ln * (cn - 1)


def front_body(
    len_ref, q_ref, tk_ref, tv_ref, k_hbm, v_hbm, par_ref, res_ref, gain_ref, wo_hbm, state_ref, normed_ref,
    kbuf, vbuf, wo, tree_mask, sbuf, half_own, half_got, attn, gath, proj, pack, blocks_got, cross_got, squares, squares_got,
    k_sem, v_sem, wo_sem, own_sem, x_send, x_recv, g_send, g_recv, b_send, b_recv, c_send, c_recv, s_send, s_recv,
    *, dims, kn, features,
):
    hn, ln, cn = dims
    n = hn * ln * cn
    hi, lo, core, _, _, _ = staged_places(*dims)
    k = lax.axis_index("kvh")
    heads, span, size = kbuf.shape
    nodes = q_ref.shape[0]
    group = q_ref.shape[1] // (heads * size)
    rows = group * nodes
    mine = nodes // cn
    part_rows = group * mine
    fb = pack.shape[1]
    per = n // kn
    factor = size**-0.5 * math.log2(math.e)
    chunk = math.gcd(span, 1024)
    to_core = lambda d: {"ffn": lax.rem(core + d, cn)}
    to_kvh = lambda d: {"kvh": lax.rem(k + d, kn)}
    flat = [(e, g, d) for e in range(hn) for g in range(ln) for d in range(cn)]

    def plane(e, g, d):
        return {"req": lax.rem(hi + e, hn) * ln + lax.rem(lo + g, ln), "ffn": lax.rem(core + d, cn)}

    meet(
        [(0, plane(*t)) for t in flat[1:]] + [(0, to_kvh(d)) for d in range(1, kn)]
    )
    k_copy = lambda h: pltpu.make_async_copy(k_hbm.at[h], kbuf.at[h], k_sem.at[h])
    v_copy = lambda h: pltpu.make_async_copy(v_hbm.at[h], vbuf.at[h], v_sem.at[h])
    wo_copy = pltpu.make_async_copy(wo_hbm, wo, wo_sem)
    for h in range(heads):
        k_copy(h).start()
        v_copy(h).start()
    wo_copy.start()
    live = jnp.clip(len_ref[lax.axis_index("req")] - core * span, 0, span)

    up = lax.broadcasted_iota(jnp.int32, (nodes, nodes), 0)
    across = lax.broadcasted_iota(jnp.int32, (nodes, nodes), 1)
    eye = jnp.where(up == across, 1.0, 0.0).astype(jnp.bfloat16)
    link = jnp.where(up == par_ref[...], 1.0, 0.0).astype(jnp.bfloat16)
    over = lax.dot_general(link, eye, (((0,), (0,)), ((), ())), preferred_element_type=jnp.float32)
    reach = jnp.minimum(over + jnp.where(up == across, 1.0, 0.0), 1.0)
    for _ in range((nodes - 1).bit_length()):
        half = reach.astype(jnp.bfloat16)
        reach = jnp.minimum(jnp.dot(half, half, preferred_element_type=jnp.float32), 1.0)
    reach = reach * jnp.where(core == 0, 1.0, 0.0)
    tree_mask[...] = jnp.concatenate(
        [reach[f * mine : (f + 1) * mine] for f in range(cn) for _ in range(group)], axis=0
    )

    def head_cols(h):
        return pl.ds(pl.multiple_of(h * size, size), size)

    def queries_of(h):
        return jnp.concatenate(
            [
                q_ref[f * mine : (f + 1) * mine, pl.ds(pl.multiple_of((h * group + g) * size, size), size)]
                for f in range(cn)
                for g in range(group)
            ],
            axis=0,
        )

    def tree_scores(h):
        s = lax.dot_general(
            queries_of(h), tk_ref[:, head_cols(h)], (((1,), (1,)), ((), ())), preferred_element_type=jnp.float32
        )
        return jnp.where(tree_mask[...] > 0.5, s, MASKED)

    def score(h):
        k_copy(h).wait()
        q = queries_of(h)
        first = kbuf[h, pl.ds(0, 16), :].astype(jnp.float32)[0:1]
        top = jnp.max(tree_scores(h), axis=1, keepdims=True)
        for c in range(span // chunk):
            spot = c * chunk + lax.broadcasted_iota(jnp.int32, (chunk, size), 0)
            keys = jnp.where(spot < live, kbuf[h, pl.ds(c * chunk, chunk), :].astype(jnp.float32), first)
            s = lax.dot_general(
                q, keys.astype(jnp.bfloat16), (((1,), (1,)), ((), ())), preferred_element_type=jnp.float32
            )
            sbuf[:, pl.ds(c * chunk, chunk)] = s
            top = jnp.maximum(top, jnp.max(s, axis=1, keepdims=True))
        half_own[h, :, pl.ds(size, size)] = jnp.broadcast_to(top, (rows, size))

    def weigh(h):
        v_copy(h).wait()
        top = half_own[h, :, pl.ds(size, 1)]
        usable = tree_mask[...] > 0.5
        w = jnp.where(usable, jnp.exp2((tree_scores(h) - top) * factor), 0.0).astype(jnp.bfloat16)
        ones = jnp.ones((nodes, size), jnp.bfloat16)
        total = jnp.dot(
            w, jnp.concatenate([tv_ref[:, head_cols(h)], ones], axis=1), preferred_element_type=jnp.float32
        )
        for c in range(span // chunk):
            spot = c * chunk + lax.broadcasted_iota(jnp.int32, (chunk, size), 0)
            usable = spot < live
            values = jnp.where(usable, vbuf[h, pl.ds(c * chunk, chunk), :].astype(jnp.float32), 0.0)
            count = jnp.where(usable, 1.0, 0.0)
            both = jnp.concatenate([values.astype(jnp.bfloat16), count.astype(jnp.bfloat16)], axis=1)
            w = jnp.exp2((sbuf[:, pl.ds(c * chunk, chunk)] - top) * factor).astype(jnp.bfloat16)
            total = total + jnp.dot(w, both, preferred_element_type=jnp.float32)
        seen = jnp.where((live > 0) | (core == 0), 1.0, 0.0)
        top = jnp.where(seen > 0.5, top * factor, MASKED)
        lane = lax.broadcasted_iota(jnp.int32, (rows, size), 1)
        half_own[h, :, pl.ds(0, size)] = total[:, :size]
        half_own[h, :, pl.ds(size, size)] = jnp.where(lane < size // 2, total[:, size:], top)
        for d in range(1, cn):
            half_copy(h, d).start()

    def part_of(f):
        return pl.ds(pl.multiple_of(f * part_rows, part_rows), part_rows)

    def half_copy(h, d):
        src = half_own.at[h, part_of(lax.rem(core + d, cn)), :]
        return remote(src, half_got.at[h, d - 1], x_send.at[h, d - 1], x_recv.at[h, d - 1], to_core(d))

    def merge(h):
        for d in range(1, cn):
            half_copy(h, d).wait_recv()
        pieces = [half_own[h, part_of(core), :]] + [half_got[h, d] for d in range(cn - 1)]
        tops = [p[:, size + size // 2 : size + size // 2 + 1] for p in pieces]
        best = functools.reduce(jnp.maximum, tops)
        above, below = 0.0, 0.0
        for p, t in zip(pieces, tops):
            scale = jnp.exp2(t - best)
            above = above + p[:, :size] * scale
            below = below + p[:, size : size + 1] * scale
        result = (above / below).astype(jnp.bfloat16)
        for g in range(group):
            attn[h, :, pl.ds(g * size, size)] = result[g * mine : (g + 1) * mine]

    start, pass_hi, pass_lo, finish, sent = token_gather(
        dims, mine, lambda h: attn.at[h], lambda h, r: gath.at[h, r, :], g_send, g_recv, own_sem
    )

    def project(h):
        wide = group * size
        piece = jnp.dot(
            gath[h], wo[pl.ds(pl.multiple_of(h * wide, wide), wide), :], preferred_element_type=jnp.float32
        )

        @pl.when(h == 0)
        def _():
            proj[...] = piece

        @pl.when(h > 0)
        def _():
            proj[...] = proj[...] + piece

    def guarded(h, *stages):
        @pl.when((h >= 0) & (h < heads))
        def _():
            for stage in stages:
                stage(h)

    def step(i, carry):
        guarded(i, score)
        guarded(i - 1, merge, start)
        guarded(i - 2, pass_hi)
        guarded(i, weigh)
        guarded(i - 2, pass_lo)

        @pl.when(i == 2)
        def _():
            wo_copy.wait()

        guarded(i - 3, finish, project)
        return carry

    lax.fori_loop(0, heads + 3, step, 0)
    pack[...] = proj[...].astype(jnp.bfloat16)

    def rows_at(e, g, d):
        b = (lax.rem(core + d, cn) * ln + lax.rem(lo + g, ln)) * hn + lax.rem(hi + e, hn)
        return pl.ds(pl.multiple_of(b * mine, mine), mine)

    def block_copy(t):
        e, g, d = flat[t]
        return remote(pack.at[rows_at(e, g, d), :], blocks_got.at[t], b_send.at[t], b_recv.at[t], plane(e, g, d))

    far_first = sorted(range(1, n), key=lambda t: -min(flat[t][0], hn - flat[t][0]))
    for t in far_first:
        block_copy(t).start()
    blocks_got[0] = pack[rows_at(0, 0, 0), :]

    def origin(b):
        f, r = lax.rem(b, cn), lax.div(b, cn)
        h, l = lax.div(r, ln), lax.rem(r, ln)
        return (lax.rem(hi + hn - h, hn) * ln + lax.rem(lo + ln - l, ln)) * cn + lax.rem(core + cn - f, cn)

    def arrived(t):
        @pl.when(t > 0)
        def _():
            remote(
                pack.at[pl.ds(0, mine), :], blocks_got.at[t], b_send.at[t], b_recv.at[t], to_core(1)
            ).wait_recv()

    def cross_copy(d, t):
        return remote(blocks_got.at[t], cross_got.at[d - 1, t], c_send.at[d - 1, t], c_recv.at[d - 1, t], to_kvh(d))

    for d in range(1, kn):

        def forward(j, carry, d=d):
            t = origin(lax.rem(k + d, kn) * per + j)
            arrived(t)
            cross_copy(d, t).start()
            return carry

        lax.fori_loop(0, per, forward, 0)

    def collect(j, square):
        t = origin(k * per + j)
        arrived(t)
        total = blocks_got[t].astype(jnp.float32)
        for d in range(1, kn):
            cross_copy(d, t).wait_recv()
            total = total + cross_got[d - 1, t].astype(jnp.float32)
        cols = pl.ds(pl.multiple_of(j * fb, fb), fb)
        total = total + res_ref[:, cols]
        state_ref[:, cols] = total
        return square + jnp.sum(total * total, axis=1, keepdims=True)

    square = lax.fori_loop(0, per, collect, jnp.zeros((mine, 1), jnp.float32))
    squares[...] = jnp.broadcast_to(square, squares.shape)

    def square_copy(d):
        return remote(squares, squares_got.at[d - 1], s_send.at[d - 1], s_recv.at[d - 1], to_kvh(d))

    for d in range(1, kn):
        square_copy(d).start()
    for d in range(1, kn):
        square_copy(d).wait_recv()
        square = square + squares_got[d - 1, :, pl.ds(0, 1)]
    scale = lax.rsqrt(square / features + EPSILON)

    def norm(j, carry):
        cols = pl.ds(pl.multiple_of(j * fb, fb), fb)
        normed_ref[:, cols] = (state_ref[:, cols] * scale * gain_ref[:, cols]).astype(jnp.bfloat16)
        return carry

    lax.fori_loop(0, per, norm, 0)
    for h in range(heads):
        sent(h)
        for d in range(1, cn):
            half_copy(h, d).wait_send()
    for t in range(1, n):
        block_copy(t).wait_send()
    for d in range(1, kn):

        def cross_sent(j, carry, d=d):
            cross_copy(d, origin(lax.rem(k + d, kn) * per + j)).wait_send()
            return carry

        lax.fori_loop(0, per, cross_sent, 0)
        square_copy(d).wait_send()


def front(queries, tree_keys, tree_values, keys, values, lengths, parents, residual, out_weight, norm_gain, collective_id):
    dims = (*split_count(lax.axis_size("req")), lax.axis_size("ffn"))
    cn, kn = dims[2], lax.axis_size("kvh")
    n = math.prod(dims)
    heads, span, size = keys.shape
    nodes, width = queries.shape
    wide = width // heads
    rows = wide // size * nodes
    mine = residual.shape[0]
    fb = out_weight.shape[1]
    links = gather_links(dims)
    vmem = pl.BlockSpec(memory_space=pltpu.VMEM)
    hbm = pl.BlockSpec(memory_space=pl.ANY)
    f32, b16 = jnp.float32, jnp.bfloat16
    dma = pltpu.SemaphoreType.DMA
    return pl.pallas_call(
        functools.partial(front_body, dims=dims, kn=kn, features=norm_gain.shape[0] * kn),
        out_shape=(jax.ShapeDtypeStruct(residual.shape, f32), jax.ShapeDtypeStruct(residual.shape, b16)),
        in_specs=[pl.BlockSpec(memory_space=pltpu.SMEM), vmem, vmem, vmem, hbm, hbm, vmem, vmem, vmem, hbm],
        out_specs=(vmem, vmem),
        scratch_shapes=[
            pltpu.VMEM((heads, span, size), b16),
            pltpu.VMEM((heads, span, size), b16),
            pltpu.VMEM(out_weight.shape, b16),
            pltpu.VMEM((rows, nodes), f32),
            pltpu.VMEM((rows, span), f32),
            pltpu.VMEM((heads, rows, 2 * size), f32),
            pltpu.VMEM((heads, cn - 1, rows // cn, 2 * size), f32),
            pltpu.VMEM((heads, mine, wide), b16),
            pltpu.VMEM((heads, n * mine, wide), b16),
            pltpu.VMEM((n * mine, fb), f32),
            pltpu.VMEM((n * mine, fb), b16),
            pltpu.VMEM((n, mine, fb), b16),
            pltpu.VMEM((kn - 1, n, mine, fb), b16),
            pltpu.VMEM((mine, 128), f32),
            pltpu.VMEM((kn - 1, mine, 128), f32),
            dma((heads,)),
            dma((heads,)),
            dma,
            dma((heads,)),
            dma((heads, cn - 1)),
            dma((heads, cn - 1)),
            dma((heads, links)),
            dma((heads, links)),
            dma((n,)),
            dma((n,)),
            dma((kn - 1, n)),
            dma((kn - 1, n)),
            dma((kn - 1,)),
            dma((kn - 1,)),
        ],
        compiler_params=pltpu.CompilerParams(
            collective_id=collective_id, has_side_effects=True, vmem_limit_bytes=63 * 1024 * 1024
        ),
    )(lengths, queries, tree_keys, tree_values, keys, values, parents, residual, norm_gain[None, :], out_weight)


def lane_block(width, most):
    return max(b for b in range(128, most + 1, 128) if width % b == 0)


def ffn_body(
    x_ref, state_ref, gate_hbm, up_hbm, down_hbm, out_ref,
    gath, wgu, wd, rbuf, part, got, act, dbuf, got_core, mid, own_mid, got_lo, low, own_low, got_hi,
    own_sem, w_sem, wd_sem, g_send, g_recv, p_send, p_recv, a_send, a_recv, c_send, c_recv, l_send, l_recv, h_send, h_recv,
    *, dims, kn, rc,
):
    hn, ln, cn = dims
    hi, lo, core, _, _, _ = staged_places(*dims)
    k = lax.axis_index("kvh")
    chunks = x_ref.shape[0] // rc
    blocks = hn * ln
    hc = wgu.shape[2] // 2
    hs = wgu.shape[0]
    total_rows = blocks * cn * rc
    keep = total_rows // kn
    fw = wd.shape[2]
    fs = x_ref.shape[1] // fw
    wd_slots, d_slots, r_slots, m_slots = wd.shape[0], dbuf.shape[0], rbuf.shape[0], own_mid.shape[0]
    to_hi = lambda d: (lax.rem(hi + d, hn), {"req": lax.rem(hi + d, hn) * ln + lo})
    to_lo = lambda d: (lax.rem(lo + d, ln), {"req": hi * ln + lax.rem(lo + d, ln)})
    to_core = lambda d: (lax.rem(core + d, cn), {"ffn": lax.rem(core + d, cn)})
    to_kvh = lambda d: (lax.rem(k + d, kn), {"kvh": lax.rem(k + d, kn)})
    meet(
        [to_hi(d) for d in range(1, hn)]
        + [to_lo(d) for d in range(1, ln)]
        + [to_core(d) for d in range(1, cn)]
        + [to_kvh(d) for d in range(1, kn)]
    )

    def weight_copies(h):
        cols = pl.ds(pl.multiple_of(h * hc, hc), hc)
        return (
            pltpu.make_async_copy(gate_hbm.at[:, cols], wgu.at[h, :, pl.ds(0, hc)], w_sem.at[0, h]),
            pltpu.make_async_copy(up_hbm.at[:, cols], wgu.at[h, :, pl.ds(hc, hc)], w_sem.at[1, h]),
        )

    def down_copy(j):
        slot = lax.rem(j, wd_slots)
        cols = pl.ds(pl.multiple_of(lax.rem(j, fs) * fw, fw), fw)
        return pltpu.make_async_copy(down_hbm.at[:, cols], wd.at[slot], wd_sem.at[slot])

    gather_start, gather_hi, gather_lo, gather_end, gather_sent = token_gather(
        dims, rc, lambda c: x_ref.at[pl.ds(c * rc, rc), :], lambda c, r: gath.at[c, r, :], g_send, g_recv, own_sem
    )

    def part_copy(s, d):
        return remote(part.at[s, d - 1], got.at[s, d - 1], p_send.at[s, d - 1], p_recv.at[s, d - 1], to_kvh(d)[1])

    def hidden(c, h):
        s = c * hs + h
        slot = lax.rem(s, r_slots)
        rbuf[slot] = jnp.dot(gath[c], wgu[h], preferred_element_type=jnp.float32)
        for d in range(1, kn):
            group = pl.ds(pl.multiple_of(to_kvh(d)[0] * keep, keep), keep)
            part[s, d - 1] = rbuf[slot, group, :].astype(jnp.bfloat16)
            part_copy(s, d).start()

    mine = pl.ds(pl.multiple_of(k * keep, keep), keep)

    def act_copy(s, d):
        c, h = lax.div(s, hs), lax.rem(s, hs)
        spot = act.at[c, mine, pl.ds(pl.multiple_of(h * hc, hc), hc)]
        return remote(spot, spot, a_send.at[s, d - 1], a_recv.at[s, d - 1], to_kvh(d)[1])

    def activate(s):
        c, h = lax.div(s, hs), lax.rem(s, hs)
        slot = lax.rem(s, r_slots)
        for d in range(1, kn):
            part_copy(s, d).wait_recv()
        gate = rbuf[slot, mine, pl.ds(0, hc)]
        up = rbuf[slot, mine, pl.ds(hc, hc)]
        for d in range(kn - 1):
            gate = gate + got[s, d, :, pl.ds(0, hc)].astype(jnp.float32)
            up = up + got[s, d, :, pl.ds(hc, hc)].astype(jnp.float32)
        act[c, mine, pl.ds(pl.multiple_of(h * hc, hc), hc)] = (gate / (1.0 + jnp.exp(-gate)) * up).astype(jnp.bfloat16)
        for d in range(1, kn):
            act_copy(s, d).start()

    def activated(c):
        def one(h, carry):
            for d in range(1, kn):
                act_copy(c * hs + h, d).wait_recv()
            return carry

        lax.fori_loop(0, hs, one, 0)

    def down_send(j, d):
        half = pl.ds(pl.multiple_of(to_core(d)[0] * (blocks * rc), blocks * rc), blocks * rc)
        return remote(
            dbuf.at[lax.rem(j, d_slots), half, :], got_core.at[j, d - 1], c_send.at[j, d - 1], c_recv.at[j, d - 1], to_core(d)[1]
        )

    def mid_send(j, d):
        return remote(mid.at[j, d - 1], got_lo.at[j, d - 1], l_send.at[j, d - 1], l_recv.at[j, d - 1], to_lo(d)[1])

    def low_send(j, d):
        return remote(low.at[j, d - 1], got_hi.at[j, d - 1], h_send.at[j, d - 1], h_recv.at[j, d - 1], to_hi(d)[1])

    def down(j):
        c = lax.div(j, fs)
        slot = lax.rem(j, d_slots)

        @pl.when(j >= d_slots)
        def _():
            for d in range(1, cn):
                down_send(j - d_slots, d).wait_send()

        down_copy(j).wait()
        dbuf[slot] = jnp.dot(act[c], wd[lax.rem(j, wd_slots)], preferred_element_type=jnp.float32)

        @pl.when(j + wd_slots < chunks * fs)
        def _():
            down_copy(j + wd_slots).start()

        for d in range(1, cn):
            down_send(j, d).start()

    def add_core(j):
        slot = lax.rem(j, d_slots)
        for d in range(1, cn):
            down_send(j, d).wait_recv()

        def total(b):
            at = pl.multiple_of(b * (hn * rc), hn * rc)
            here = pl.multiple_of(core * (blocks * rc), blocks * rc) + at
            result = dbuf[slot, pl.ds(pl.multiple_of(here, hn * rc), hn * rc), :]
            for d in range(cn - 1):
                result = result + got_core[j, d, pl.ds(at, hn * rc), :]
            return result

        for d in range(1, ln):
            mid[j, d - 1] = total(to_lo(d)[0]).astype(jnp.bfloat16)
            mid_send(j, d).start()
        own_mid[lax.rem(j, m_slots)] = total(lo)

    def add_lo(j):
        slot = lax.rem(j, m_slots)
        for d in range(1, ln):
            mid_send(j, d).wait_recv()

        def total(h):
            at = pl.ds(pl.multiple_of(h * rc, rc), rc)
            result = own_mid[slot, at, :]
            for d in range(ln - 1):
                result = result + got_lo[j, d, at, :].astype(jnp.float32)
            return result

        for d in range(1, hn):
            low[j, d - 1] = total(to_hi(d)[0]).astype(jnp.bfloat16)
            low_send(j, d).start()
        own_low[slot] = total(hi)

    def add_hi(j):
        c, n = lax.div(j, fs), lax.rem(j, fs)
        for d in range(1, hn):
            low_send(j, d).wait_recv()
        result = own_low[lax.rem(j, m_slots)]
        for d in range(hn - 1):
            result = result + got_hi[j, d].astype(jnp.float32)
        at = (pl.ds(pl.multiple_of(c * rc, rc), rc), pl.ds(pl.multiple_of(n * fw, fw), fw))
        out_ref[at] = state_ref[at] + result

    pieces = chunks * fs
    lag = 2

    def piece(j):
        for depth, stage in enumerate((down, add_core, add_lo, add_hi)):

            @pl.when((j >= depth * lag) & (j < pieces + depth * lag))
            def _(depth=depth, stage=stage):
                stage(j - depth * lag)

    for h in range(hs):
        for copy in weight_copies(h):
            copy.start()
    for j in range(min(wd_slots, pieces)):
        down_copy(j).start()
    gather_start(0)
    gather_hi(0)
    gather_lo(0)
    for c in range(1, chunks):
        gather_start(c)
    gather_end(0)
    behind = 2
    marks = {3: gather_hi, 5: gather_lo, hs - 1: gather_end}
    per = -(-fs // (hs - 3))
    for c in range(chunks):

        def step(h, carry, c=c):
            if c == 0:
                for copy in weight_copies(h):
                    copy.wait()
            hidden(c, h)

            @pl.when(c * hs + h >= behind)
            def _():
                activate(c * hs + h - behind)

            if c + 1 < chunks:
                for at, stage in marks.items():

                    @pl.when(h == at)
                    def _(stage=stage):
                        stage(c + 1)

            if c > 0:

                @pl.when(h == 3)
                def _():
                    activated(c - 1)

                @pl.when(h >= 3)
                def _():
                    def one(i, carry):
                        piece((c - 1) * fs + (h - 3) * per + i)
                        return carry

                    lax.fori_loop(0, jnp.minimum(per, fs - (h - 3) * per), one, 0)

            return carry

        lax.fori_loop(0, hs, step, 0)
    for s in range(chunks * hs - behind, chunks * hs):
        activate(s)
    activated(chunks - 1)

    def last(j, carry):
        piece(j)
        return carry

    lax.fori_loop((chunks - 1) * fs, pieces + 3 * lag, last, 0)
    for c in range(chunks):
        gather_sent(c)

    def sent_steps(s, carry):
        for d in range(1, kn):
            part_copy(s, d).wait_send()
            act_copy(s, d).wait_send()
        return carry

    lax.fori_loop(0, chunks * hs, sent_steps, 0)

    def sent_pieces(j, carry):
        @pl.when(j >= pieces - d_slots)
        def _():
            for d in range(1, cn):
                down_send(j, d).wait_send()

        for d in range(1, ln):
            mid_send(j, d).wait_send()
        for d in range(1, hn):
            low_send(j, d).wait_send()
        return carry

    lax.fori_loop(0, pieces, sent_pieces, 0)


def feed_forward(x, state, gate_weight, up_weight, down_weight, collective_id):
    hn, ln = split_count(lax.axis_size("req"))
    cn, kn = lax.axis_size("ffn"), lax.axis_size("kvh")
    rows, width = x.shape
    rc = math.gcd(rows, 16)
    chunks = rows // rc
    hidden = gate_weight.shape[1]
    hc = lane_block(hidden, 256)
    hs = hidden // hc
    fw = lane_block(width, max(128, width // 8))
    pieces = chunks * (width // fw)
    tokens = hn * ln * cn * rc
    keep = tokens // kn
    links = gather_links((hn, ln, cn))
    vmem = pl.BlockSpec(memory_space=pltpu.VMEM)
    hbm = pl.BlockSpec(memory_space=pl.ANY)
    f32, b16 = jnp.float32, jnp.bfloat16
    dma = pltpu.SemaphoreType.DMA
    steps = chunks * hs
    return pl.pallas_call(
        functools.partial(ffn_body, dims=(hn, ln, cn), kn=kn, rc=rc),
        out_shape=jax.ShapeDtypeStruct(state.shape, f32),
        in_specs=[vmem, vmem, hbm, hbm, hbm],
        out_specs=vmem,
        scratch_shapes=[
            pltpu.VMEM((chunks, tokens, width), b16),
            pltpu.VMEM((hs, width, 2 * hc), b16),
            pltpu.VMEM((3, hidden, fw), b16),
            pltpu.VMEM((3, tokens, 2 * hc), f32),
            pltpu.VMEM((steps, kn - 1, keep, 2 * hc), b16),
            pltpu.VMEM((steps, kn - 1, keep, 2 * hc), b16),
            pltpu.VMEM((chunks, tokens, hidden), b16),
            pltpu.VMEM((4, tokens, fw), f32),
            pltpu.VMEM((pieces, cn - 1, hn * ln * rc, fw), f32),
            pltpu.VMEM((pieces, ln - 1, hn * rc, fw), b16),
            pltpu.VMEM((4, hn * rc, fw), f32),
            pltpu.VMEM((pieces, ln - 1, hn * rc, fw), b16),
            pltpu.VMEM((pieces, hn - 1, rc, fw), b16),
            pltpu.VMEM((4, rc, fw), f32),
            pltpu.VMEM((pieces, hn - 1, rc, fw), b16),
            dma((chunks,)),
            dma((2, hs)),
            dma((3,)),
            dma((chunks, links)),
            dma((chunks, links)),
            dma((steps, kn - 1)),
            dma((steps, kn - 1)),
            dma((steps, kn - 1)),
            dma((steps, kn - 1)),
            dma((pieces, cn - 1)),
            dma((pieces, cn - 1)),
            dma((pieces, ln - 1)),
            dma((pieces, ln - 1)),
            dma((pieces, hn - 1)),
            dma((pieces, hn - 1)),
        ],
        compiler_params=pltpu.CompilerParams(
            collective_id=collective_id, has_side_effects=True, vmem_limit_bytes=63 * 1024 * 1024
        ),
    )(x, state, gate_weight, up_weight, down_weight)


def local(
    queries,
    tree_keys,
    tree_token_values,
    cache_keys,
    cached_value_rows,
    lengths,
    parents,
    residual,
    out_weight,
    norm_gain,
    gate_weight,
    up_weight,
    down_weight,
):
    state, normed = front(
        queries[0],
        tree_keys[0],
        tree_token_values[0],
        cache_keys[0],
        cached_value_rows[0],
        lengths,
        parents,
        residual,
        out_weight,
        norm_gain,
        1,
    )
    return feed_forward(normed, state, gate_weight, up_weight, down_weight, 2)


def solution(mesh):
    in_specs = (
        P("req", None, "kvh"),
        P("req", None, "kvh"),
        P("req", None, "kvh"),
        P("req", "kvh", "ffn", None),
        P("req", "kvh", "ffn", None),
        P(),
        P("req", None),
        P(("req", "ffn"), "kvh"),
        P("kvh", ("req", "ffn")),
        P("kvh"),
        P("kvh", ("req", "ffn")),
        P("kvh", ("req", "ffn")),
        P(("req", "ffn"), "kvh"),
    )
    out_specs = P(("req", "ffn"), "kvh")
    return jax.shard_map(local, mesh=mesh, in_specs=in_specs, out_specs=out_specs, check_vma=False)
```

```python
import functools
import math

import jax
import jax.numpy as jnp
from jax import lax
from jax.experimental import pallas as pl
from jax.experimental.pallas import tpu as pltpu
from jax.sharding import PartitionSpec as P

MASKED = -1e30
EPSILON = 1e-05
MESH = pl.DeviceIdType.MESH
ROWS = 16
LAG = 4
BEHIND = 4
PARTS = 8


def split_count(n):
    lo = math.isqrt(n)
    while n % lo:
        lo -= 1
    return n // lo, lo


def lane_block(width, most):
    return max(b for b in range(128, most + 1, 128) if width % b == 0)


def remote(src, dst, send, recv, where):
    return pltpu.make_async_remote_copy(
        src_ref=src, dst_ref=dst, send_sem=send, recv_sem=recv, device_id=where, device_id_type=MESH
    )


class Gather:
    def __init__(self, dims, line, source, target, sems):
        self.dims, self.line, self.source, self.target = dims, line, source, target
        self.z_send, self.z_recv, self.y_send, self.y_recv, self.c_send, self.c_recv, self.own_sem = sems
        req = lax.axis_index("req")
        self.hi, self.lo, self.core = req // dims[1], lax.rem(req, dims[1]), lax.axis_index("ffn")

    def place(self, c, o, g, f=None):
        hn, ln, cn = self.dims
        f = self.core if f is None else f
        return self.target(c, (f * ln + lax.rem(self.lo + ln - g, ln)) * hn + o, f)

    def z_copy(self, c, o, up):
        step = 1 if up else -1
        where = {"req": (self.hi + step) * self.dims[1] + self.lo}
        spot = self.place(c, o, 0)
        return remote(spot, spot, self.z_send.at[c, 0 if up else 1, o], self.z_recv.at[c, o], where)

    def z_own(self, c, up):
        step = 1 if up else -1
        where = {"req": (self.hi + step) * self.dims[1] + self.lo}
        o = self.hi
        return remote(
            self.source(c), self.place(c, o, 0), self.z_send.at[c, 0 if up else 1, o], self.z_recv.at[c, o], where
        )

    def z_far(self, c, e, up):
        o = self.hi
        where = {"req": (o + (e if up else -e)) * self.dims[1] + self.lo}
        at = 0 if up else 1
        return remote(self.source(c), self.place(c, o, 0), self.z_send.at[c, at, e], self.z_recv.at[c, o], where)

    def far(self, body):
        for e in range(1, self.dims[0]):

            @pl.when(self.hi + e < self.dims[0])
            def _(e=e):
                body(e, True)

            @pl.when(self.hi >= e)
            def _(e=e):
                body(e, False)

    def y_copy(self, c, o, d, own=False):
        ln = self.dims[1]
        where = {"req": self.hi * ln + lax.rem(self.lo + d, ln)}
        src = self.source(c) if own else self.place(c, o, 0)
        return remote(src, self.place(c, o, 0), self.y_send.at[c, o, d - 1], self.y_recv.at[c, o, d - 1], where)

    def c_copy(self, c, o, g, d, own=False):
        where = {"ffn": lax.rem(self.core + d, self.dims[2])}
        src = self.source(c) if own else self.place(c, o, g)
        at = o * self.dims[1] + g
        return remote(src, self.place(c, o, g), self.c_send.at[c, at, d - 1], self.c_recv.at[c, at, d - 1], where)

    def own_copy(self, c):
        return pltpu.make_async_copy(self.source(c), self.place(c, self.hi, 0), self.own_sem.at[c])

    def around(self, e, body):
        @pl.when(self.hi >= e)
        def _():
            body(self.hi - e, True)

        @pl.when(self.hi + e < self.dims[0])
        def _():
            body(self.hi + e, False)

    def onward(self, up, body):
        @pl.when(self.hi + 1 < self.dims[0] if up else self.hi > 0)
        def _():
            body()

    def start(self, c):
        hn, ln, cn = self.dims
        if self.line:
            for up in (True, False):
                self.onward(up, lambda up=up: self.z_own(c, up).start())
        else:
            self.far(lambda e, up: self.z_far(c, e, up).start())
        for d in range(1, ln):
            self.y_copy(c, self.hi, d, True).start()
        for d in range(1, cn):
            self.c_copy(c, self.hi, 0, d, True).start()
        self.own_copy(c).start()

    def pass_hi(self, c, reach=None):
        hn, ln, cn = self.dims

        def one(o, up):
            self.z_copy(c, o, up).wait_recv()
            if self.line:
                self.onward(up, lambda: self.z_copy(c, o, up).start())
            for d in range(1, ln):
                self.y_copy(c, o, d).start()
            for d in range(1, cn):
                self.c_copy(c, o, 0, d).start()

        for e in range(1, hn) if reach is None else [reach]:
            self.around(e, one)

    def pass_lo(self, c):
        hn, ln, cn = self.dims

        def one(o, up):
            for g in range(1, ln):
                self.y_copy(c, o, g).wait_recv()
                for d in range(1, cn):
                    self.c_copy(c, o, g, d).start()

        one(self.hi, True)
        for e in range(1, hn):
            self.around(e, one)

    def take(self, c, d, parts=None):
        hn, ln, cn = self.dims
        for g in range(ln) if parts is None else parts:
            for o in range(hn):
                self.c_copy(c, o, g, d).wait_recv()

    def sent(self, c):
        hn, ln, cn = self.dims
        if self.line:
            for up in (True, False):
                self.onward(up, lambda up=up: self.z_own(c, up).wait_send())
            for e in range(1, hn):
                self.around(e, lambda o, up: self.onward(up, lambda: self.z_copy(c, o, up).wait_send()))
        else:
            self.far(lambda e, up: self.z_far(c, e, up).wait_send())
        for o in range(hn):
            for d in range(1, ln):
                self.y_copy(c, o, d).wait_send()
            for g in range(ln):
                for d in range(1, cn):
                    self.c_copy(c, o, g, d).wait_send()


def gather_sems(count, dims):
    hn, ln, cn = dims
    dma = pltpu.SemaphoreType.DMA
    return [
        dma((count, 2, hn)),
        dma((count, hn)),
        dma((count, hn, max(ln - 1, 1))),
        dma((count, hn, max(ln - 1, 1))),
        dma((count, hn * ln, max(cn - 1, 1))),
        dma((count, hn * ln, max(cn - 1, 1))),
        dma((count,)),
    ]


def layer_body(
    len_ref, q_ref, tk_ref, tv_ref, k_hbm, v_hbm, par_ref, res_hbm, gain_ref, wo_hbm, gate_hbm, up_hbm, down_hbm, out_ref,
    gath, state, normed, half_got, pack, blocks_got, cross_got, squares, squares_got,
    rbuf, part, got, act, dbuf, got_core, mid, own_mid, got_lo, low, own_low, got_hi,
    k_sem, v_sem, wo_sem, res_sem, w_sem, wd_sem,
    a0, a1, a2, a3, a4, a5, a6, d0, d1, d2, d3, d4, d5, d6,
    x_send, x_recv, b_send, b_recv, f_send, f_recv, s_send, s_recv,
    p_send, p_recv, a_send, a_recv, c_send, c_recv, l_send, l_recv, h_send, h_recv,
    *, dims, kn, heads, hc, fw,
):
    hn, ln, cn = dims
    n = hn * ln * cn
    req = lax.axis_index("req")
    hi, lo, core, k = req // ln, lax.rem(req, ln), lax.axis_index("ffn"), lax.axis_index("kvh")
    span, size = k_hbm.shape[1:]
    nodes = q_ref.shape[0]
    group = q_ref.shape[1] // (heads * size)
    wide = group * size
    rows = group * nodes
    mine = nodes // cn
    part_rows = group * mine
    fb = pack.shape[1]
    per = n // kn
    width = normed.shape[1]
    features = width * kn
    factor = size**-0.5 * math.log2(math.e)
    chunk = math.gcd(span, 1024)
    hidden_width = act.shape[2]
    hs = hidden_width // hc
    fs = width // fw
    to_hi = lambda d: {"req": lax.rem(hi + d, hn) * ln + lo}
    to_lo = lambda d: {"req": hi * ln + lax.rem(lo + d, ln)}
    to_core = lambda d: {"ffn": lax.rem(core + d, cn)}
    to_kvh = lambda d: {"kvh": lax.rem(k + d, kn)}
    flat = [(e, g, d) for e in range(hn) for g in range(ln) for d in range(cn)]

    def plane(e, g, d):
        return {"req": lax.rem(hi + e, hn) * ln + lax.rem(lo + g, ln), "ffn": lax.rem(core + d, cn)}

    barrier = pltpu.get_barrier_semaphore()
    peers = [plane(*t) for t in flat[1:]] + [to_kvh(d) for d in range(1, kn)]
    for where in peers:
        pl.semaphore_signal(barrier, inc=1, device_id=where, device_id_type=MESH)

    def attention_phase(kbuf, vbuf, wo, sbuf, tree_mask, half_own, attn, proj):
        k_copy = lambda h: pltpu.make_async_copy(k_hbm.at[h], kbuf.at[h], k_sem.at[h])
        v_copy = lambda h: pltpu.make_async_copy(v_hbm.at[h], vbuf.at[h], v_sem.at[h])
        wo_copy = pltpu.make_async_copy(wo_hbm, wo, wo_sem)
        for h in range(heads):
            k_copy(h).start()
            v_copy(h).start()
        wo_copy.start()
        pltpu.make_async_copy(res_hbm, state, res_sem).start()
        live = jnp.clip(len_ref[lax.axis_index("req")] - core * span, 0, span)

        up = lax.broadcasted_iota(jnp.int32, (nodes, nodes), 0)
        across = lax.broadcasted_iota(jnp.int32, (nodes, nodes), 1)
        eye = jnp.where(up == across, 1.0, 0.0).astype(jnp.bfloat16)
        link = jnp.where(up == par_ref[...], 1.0, 0.0).astype(jnp.bfloat16)
        over = lax.dot_general(link, eye, (((0,), (0,)), ((), ())), preferred_element_type=jnp.float32)
        reach = jnp.minimum(over + jnp.where(up == across, 1.0, 0.0), 1.0)
        for _ in range((nodes - 1).bit_length()):
            half = reach.astype(jnp.bfloat16)
            reach = jnp.minimum(jnp.dot(half, half, preferred_element_type=jnp.float32), 1.0)
        reach = reach * jnp.where(core == 0, 1.0, 0.0)
        tree_mask[...] = jnp.concatenate(
            [reach[f * mine : (f + 1) * mine] for f in range(cn) for _ in range(group)], axis=0
        )
        def head_cols(h):
            return pl.ds(pl.multiple_of(h * size, size), size)

        def queries_of(h):
            return jnp.concatenate(
                [
                    q_ref[f * mine : (f + 1) * mine, pl.ds(pl.multiple_of((h * group + g) * size, size), size)]
                    for f in range(cn)
                    for g in range(group)
                ],
                axis=0,
            )

        def tree_scores(h):
            s = lax.dot_general(
                queries_of(h), tk_ref[:, head_cols(h)], (((1,), (1,)), ((), ())), preferred_element_type=jnp.float32
            )
            return jnp.where(tree_mask[...] > 0.5, s, MASKED)

        def score(h):
            k_copy(h).wait()
            q = queries_of(h)
            first = kbuf[h, pl.ds(0, 16), :].astype(jnp.float32)[0:1]
            top = jnp.max(tree_scores(h), axis=1, keepdims=True)
            for c in range(span // chunk):
                spot = c * chunk + lax.broadcasted_iota(jnp.int32, (chunk, size), 0)
                keys = jnp.where(spot < live, kbuf[h, pl.ds(c * chunk, chunk), :].astype(jnp.float32), first)
                s = lax.dot_general(
                    q, keys.astype(jnp.bfloat16), (((1,), (1,)), ((), ())), preferred_element_type=jnp.float32
                )
                sbuf[:, pl.ds(c * chunk, chunk)] = s
                top = jnp.maximum(top, jnp.max(s, axis=1, keepdims=True))
            half_own[h, :, pl.ds(size, size)] = jnp.broadcast_to(top, (rows, size))

        def weigh(h):
            v_copy(h).wait()
            top = half_own[h, :, pl.ds(size, 1)]
            usable = tree_mask[...] > 0.5
            w = jnp.where(usable, jnp.exp2((tree_scores(h) - top) * factor), 0.0).astype(jnp.bfloat16)
            ones = jnp.ones((nodes, size), jnp.bfloat16)
            total = jnp.dot(
                w, jnp.concatenate([tv_ref[:, head_cols(h)], ones], axis=1), preferred_element_type=jnp.float32
            )
            for c in range(span // chunk):
                spot = c * chunk + lax.broadcasted_iota(jnp.int32, (chunk, size), 0)
                usable = spot < live
                values = jnp.where(usable, vbuf[h, pl.ds(c * chunk, chunk), :].astype(jnp.float32), 0.0)
                count = jnp.where(usable, 1.0, 0.0)
                both = jnp.concatenate([values.astype(jnp.bfloat16), count.astype(jnp.bfloat16)], axis=1)
                w = jnp.exp2((sbuf[:, pl.ds(c * chunk, chunk)] - top) * factor).astype(jnp.bfloat16)
                total = total + jnp.dot(w, both, preferred_element_type=jnp.float32)
            seen = jnp.where((live > 0) | (core == 0), 1.0, 0.0)
            top = jnp.where(seen > 0.5, top * factor, MASKED)
            lane = lax.broadcasted_iota(jnp.int32, (rows, size), 1)
            half_own[h, :, pl.ds(0, size)] = total[:, :size]
            half_own[h, :, pl.ds(size, size)] = jnp.where(lane < size // 2, total[:, size:], top)
            for d in range(1, cn):
                half_copy(h, d).start()
        def part_of(f):
            return pl.ds(pl.multiple_of(f * part_rows, part_rows), part_rows)

        def half_copy(h, d):
            src = half_own.at[h, part_of(lax.rem(core + d, cn)), :]
            return remote(src, half_got.at[h, d - 1], x_send.at[h, d - 1], x_recv.at[h, d - 1], to_core(d))

        def merge(h):
            for d in range(1, cn):
                half_copy(h, d).wait_recv()
            pieces = [half_own[h, part_of(core), :]] + [half_got[h, d] for d in range(cn - 1)]
            tops = [p[:, size + size // 2 : size + size // 2 + 1] for p in pieces]
            best = functools.reduce(jnp.maximum, tops)
            above, below = 0.0, 0.0
            for p, t in zip(pieces, tops):
                scale = jnp.exp2(t - best)
                above = above + p[:, :size] * scale
                below = below + p[:, size : size + 1] * scale
            result = (above / below).astype(jnp.bfloat16)
            for g in range(group):
                attn[h, :, pl.ds(g * size, size)] = result[g * mine : (g + 1) * mine]
        gather = Gather(
            dims,
            True,
            lambda h: attn.at[h],
            lambda h, b, f: gath.at[
                pl.ds(pl.multiple_of(b * mine, mine), mine), pl.ds(pl.multiple_of(h * wide, wide), wide)
            ],
            (a0, a1, a2, a3, a4, a5, a6),
        )

        def finish(h):
            for d in range(1, cn):
                gather.take(h, d)
            gather.own_copy(h).wait()

        def project(h):
            cols = pl.ds(pl.multiple_of(h * wide, wide), wide)
            piece = jnp.dot(gath[:, cols], wo[cols, :], preferred_element_type=jnp.float32)

            @pl.when(h == 0)
            def _():
                proj[...] = piece

            @pl.when(h > 0)
            def _():
                proj[...] = proj[...] + piece

        def guarded(h, *stages):
            @pl.when((h >= 0) & (h < heads))
            def _():
                for stage in stages:
                    with jax.named_scope(stage.__name__):
                        stage(h)

        def step(i, carry):
            guarded(i, score)

            @pl.when(i == 0)
            def _():
                with jax.named_scope("barrier_wait"):
                    pl.semaphore_wait(barrier, len(peers))

            guarded(i - 1, merge, gather.start)
            for e in range(1, hn):

                def pass_hi(h, e=e):
                    gather.pass_hi(h, e)

                guarded(i - 1 - e, pass_hi)
            guarded(i, weigh)
            guarded(i - 1 - hn, gather.pass_lo)

            @pl.when(i == 2)
            def _():
                wo_copy.wait()

            guarded(i - 2 - hn, finish, project)
            return carry

        lax.fori_loop(0, heads + 2 + hn, step, 0)
        pack[...] = proj[...].astype(jnp.bfloat16)

        def sent(h, carry):
            gather.sent(h)
            for d in range(1, cn):
                half_copy(h, d).wait_send()
            return carry

        lax.fori_loop(0, heads, sent, 0)

    def forward_phase(wgu, wd):
        wd_slots, r_slots, m_slots, t_slots = wd.shape[0], rbuf.shape[0], own_mid.shape[0], dbuf.shape[0] - fs
        chunks = mine // ROWS
        items = chunks * cn
        steps = items * hs
        loads = (chunks - 1 + cn) * fs
        tokens = n // cn * ROWS
        keep = tokens // kn
        half_rows = hn * ROWS

        def weight_copies(h):
            cols = pl.ds(pl.multiple_of(h * hc, hc), hc)
            return (
                pltpu.make_async_copy(gate_hbm.at[:, cols], wgu.at[h, :, pl.ds(0, hc)], w_sem.at[0, h]),
                pltpu.make_async_copy(up_hbm.at[:, cols], wgu.at[h, :, pl.ds(hc, hc)], w_sem.at[1, h]),
            )

        def down_copy(j):
            slot = lax.rem(j, wd_slots)
            cols = pl.ds(pl.multiple_of(lax.rem(j, fs) * fw, fw), fw)
            return pltpu.make_async_copy(down_hbm.at[:, cols], wd.at[slot], wd_sem.at[slot])

        for h in range(hs):
            for copy in weight_copies(h):
                copy.start()
        for j in range(min(wd_slots, loads)):
            down_copy(j).start()
        def rows_at(e, g, d):
            b = (lax.rem(core + d, cn) * ln + lax.rem(lo + g, ln)) * hn + lax.rem(hi + e, hn)
            return pl.ds(pl.multiple_of(b * mine, mine), mine)

        def block_copy(t):
            e, g, d = flat[t]
            return remote(pack.at[rows_at(e, g, d), :], blocks_got.at[t], b_send.at[t], b_recv.at[t], plane(e, g, d))

        far_first = sorted(range(1, n), key=lambda t: -min(flat[t][0], hn - flat[t][0]))
        for t in far_first:
            block_copy(t).start()
        blocks_got[0] = pack[rows_at(0, 0, 0), :]

        def origin(b):
            f, r = lax.rem(b, cn), lax.div(b, cn)
            h, l = lax.div(r, ln), lax.rem(r, ln)
            return (lax.rem(hi + hn - h, hn) * ln + lax.rem(lo + ln - l, ln)) * cn + lax.rem(core + cn - f, cn)

        def arrived(t):
            @pl.when(t > 0)
            def _():
                remote(
                    pack.at[pl.ds(0, mine), :], blocks_got.at[t], b_send.at[t], b_recv.at[t], to_core(1)
                ).wait_recv()

        def cross_copy(d, t):
            return remote(blocks_got.at[t], cross_got.at[d - 1, t], f_send.at[d - 1, t], f_recv.at[d - 1, t], to_kvh(d))

        for d in range(1, kn):

            def forward(j, carry, d=d):
                t = origin(lax.rem(k + d, kn) * per + j)
                arrived(t)
                cross_copy(d, t).start()
                return carry

            with jax.named_scope("forward"):
                lax.fori_loop(0, per, forward, 0)

        def collect(j, square):
            t = origin(k * per + j)
            arrived(t)
            total = blocks_got[t].astype(jnp.float32)
            for d in range(1, kn):
                cross_copy(d, t).wait_recv()
                total = total + cross_got[d - 1, t].astype(jnp.float32)
            cols = pl.ds(pl.multiple_of(j * fb, fb), fb)
            total = total + state[:, cols]
            state[:, cols] = total
            return square + jnp.sum(total * total, axis=1, keepdims=True)

        pltpu.make_async_copy(res_hbm, state, res_sem).wait()
        with jax.named_scope("collect"):
            square = lax.fori_loop(0, per, collect, jnp.zeros((mine, 1), jnp.float32))
        squares[...] = jnp.broadcast_to(square, squares.shape)

        def square_copy(d):
            return remote(squares, squares_got.at[d - 1], s_send.at[d - 1], s_recv.at[d - 1], to_kvh(d))

        for d in range(1, kn):
            square_copy(d).start()
        for d in range(1, kn):
            square_copy(d).wait_recv()
            square = square + squares_got[d - 1, :, pl.ds(0, 1)]
        scale = lax.rsqrt(square / features + EPSILON)

        def norm(j, carry):
            cols = pl.ds(pl.multiple_of(j * fb, fb), fb)
            normed[:, cols] = (state[:, cols] * scale * gain_ref[:, cols]).astype(jnp.bfloat16)
            return carry

        lax.fori_loop(0, per, norm, 0)
        gather = Gather(
            dims,
            False,
            lambda c: normed.at[pl.ds(pl.multiple_of(c * ROWS, ROWS), ROWS), :],
            lambda c, b, f: gath.at[pl.ds(pl.multiple_of(c * (n * ROWS) + b * ROWS, ROWS), ROWS), :],
            (d0, d1, d2, d3, d4, d5, d6),
        )

        def mine_of(item):
            return core == lax.rem(item, cn)

        def on_owner(item, stage):
            @pl.when(mine_of(item))
            def _():
                stage(lax.div(item, cn))

        def ready(item, own=True, parts=None):
            c = lax.div(item, cn)
            if own:

                @pl.when(mine_of(item))
                def _():
                    gather.own_copy(c).wait()

            for d in range(1, cn):

                @pl.when(lax.rem(core + cn - d, cn) == lax.rem(item, cn))
                def _(d=d):
                    gather.take(c, d, parts)

        item_rows = lambda item: pl.ds(pl.multiple_of(item * tokens, tokens), tokens)
        mine_rows = pl.ds(pl.multiple_of(k * keep, keep), keep)

        def part_copy(s, d):
            return remote(part.at[lax.rem(s, PARTS), d - 1], got.at[s, d - 1], p_send.at[s, d - 1], p_recv.at[s, d - 1], to_kvh(d))

        def hidden(s):
            item, h = lax.div(s, hs), lax.rem(s, hs)
            slot = lax.rem(s, r_slots)
            rbuf[slot] = jnp.dot(gath[item_rows(item), :], wgu[h], preferred_element_type=jnp.float32)
            for d in range(1, kn):

                @pl.when(s >= PARTS)
                def _(d=d):
                    part_copy(s - PARTS, d).wait_send()

                theirs = pl.ds(pl.multiple_of(lax.rem(k + d, kn) * keep, keep), keep)
                part[lax.rem(s, PARTS), d - 1] = rbuf[slot, theirs, :].astype(jnp.bfloat16)
                part_copy(s, d).start()

        def act_copy(s, d):
            item, h = lax.div(s, hs), lax.rem(s, hs)
            spot = act.at[item, mine_rows, pl.ds(pl.multiple_of(h * hc, hc), hc)]
            return remote(spot, spot, a_send.at[s, d - 1], a_recv.at[s, d - 1], to_kvh(d))

        def activate(s):
            item, h = lax.div(s, hs), lax.rem(s, hs)
            slot = lax.rem(s, r_slots)
            for d in range(1, kn):
                part_copy(s, d).wait_recv()
            gate = rbuf[slot, mine_rows, pl.ds(0, hc)]
            up = rbuf[slot, mine_rows, pl.ds(hc, hc)]
            for d in range(kn - 1):
                gate = gate + got[s, d, :, pl.ds(0, hc)].astype(jnp.float32)
                up = up + got[s, d, :, pl.ds(hc, hc)].astype(jnp.float32)
            value = (gate / (1.0 + jnp.exp(-gate)) * up).astype(jnp.bfloat16)
            act[item, mine_rows, pl.ds(pl.multiple_of(h * hc, hc), hc)] = value
            for d in range(1, kn):
                act_copy(s, d).start()

        def activated(item):
            def one(h, carry):
                for d in range(1, kn):
                    act_copy(item * hs + h, d).wait_recv()
                return carry

            lax.fori_loop(0, hs, one, 0)

        def kept(item, i):
            return lax.div(item, cn) * fs + i

        def down_slot(item, i):
            j = kept(item, i)
            return jnp.where(mine_of(item), lax.rem(j, fs), fs + lax.rem(j, t_slots))

        def down_send(item, i, d):
            j = kept(item, i)
            return remote(
                dbuf.at[fs + lax.rem(j, t_slots)], got_core.at[j, d - 1], c_send.at[d - 1, j], c_recv.at[j, d - 1], to_core(d)
            )

        def each_core(item, body):
            for d in range(1, cn):

                @pl.when(lax.rem(core + d, cn) == lax.rem(item, cn))
                def _(d=d):
                    body(d)

        def multiply(load, members, i):
            down_copy(load).wait()
            for item in members:

                @pl.when(kept(item, i) >= t_slots)
                def _(item=item):
                    each_core(item, lambda d: down_send(item, i - t_slots, d).wait_send())

                dbuf[down_slot(item, i)] = jnp.dot(
                    act[item], wd[lax.rem(load, wd_slots)], preferred_element_type=jnp.float32
                )
                each_core(item, lambda d: down_send(item, i, d).start())

            @pl.when(load + wd_slots < loads)
            def _():
                down_copy(load + wd_slots).start()

        def mid_send(item, i, d):
            j = kept(item, i)
            return remote(mid.at[j, d - 1], got_lo.at[j, d - 1], l_send.at[j, d - 1], l_recv.at[j, d - 1], to_lo(d))

        def low_send(item, i, d):
            j = kept(item, i)
            return remote(low.at[j, d - 1], got_hi.at[j, d - 1], h_send.at[j, d - 1], h_recv.at[j, d - 1], to_hi(d))

        def add_core(item, i):
            j = kept(item, i)
            slot = lax.rem(j, fs)
            for d in range(1, cn):
                down_send(item, i, d).wait_recv()

            def total(b):
                at = pl.ds(pl.multiple_of(b * half_rows, half_rows), half_rows)
                result = dbuf[slot, at, :]
                for d in range(cn - 1):
                    result = result + got_core[j, d, at, :]
                return result

            for d in range(1, ln):
                mid[j, d - 1] = total(lax.rem(lo + d, ln)).astype(jnp.bfloat16)
                mid_send(item, i, d).start()
            own_mid[lax.rem(j, m_slots)] = total(lo)

        def add_lo(item, i):
            j = kept(item, i)
            slot = lax.rem(j, m_slots)
            for d in range(1, ln):
                mid_send(item, i, d).wait_recv()

            def total(h):
                at = pl.ds(pl.multiple_of(h * ROWS, ROWS), ROWS)
                result = own_mid[slot, at, :]
                for d in range(ln - 1):
                    result = result + got_lo[j, d, at, :].astype(jnp.float32)
                return result

            for d in range(1, hn):
                low[j, d - 1] = total(lax.rem(hi + d, hn)).astype(jnp.bfloat16)
                low_send(item, i, d).start()
            own_low[j] = total(hi)

        def add_hi(item, i):
            j = kept(item, i)
            c = lax.div(item, cn)
            for d in range(1, hn):
                low_send(item, i, d).wait_recv()
            result = own_low[j]
            for d in range(hn - 1):
                result = result + got_hi[j, d].astype(jnp.float32)
            at = (pl.ds(pl.multiple_of(c * ROWS, ROWS), ROWS), pl.ds(pl.multiple_of(i * fw, fw), fw))
            out_ref[at] = state[at] + result

        def within(i, stage, *args):
            @pl.when((i >= 0) & (i < fs))
            def _():
                with jax.named_scope(stage.__name__.strip('<>')):
                    stage(*args, i)

        def down_all(c, i):
            within(i, lambda i: multiply(c * fs + i, [c * cn + f for f in range(cn)], i))

        def down_one(item, i):
            within(i, lambda i: multiply((chunks - 1 + lax.rem(item, cn)) * fs + i, [item], i))

        def owned(item, i, stage):
            @pl.when(mine_of(item))
            def _():
                within(i, stage, item)

        def stretch(at, first, per_step, stage):
            @pl.when((at >= first) & (at - first < -(-fs // per_step)))
            def _():
                def one(i, carry):
                    stage((at - first) * per_step + i)
                    return carry

                lax.fori_loop(0, per_step, one, 0)

        on_owner(0, gather.start)
        with jax.named_scope("first_hi"):
            on_owner(0, gather.pass_hi)
        with jax.named_scope("first_lo"):
            on_owner(0, gather.pass_lo)
        with jax.named_scope("first_ready"):
            ready(0, False, range(1))
            for f in range(1, cn):
                on_owner(f, gather.start)
            ready(0, True, range(1, ln))

        def step(s, carry):
            item, h = lax.div(s, hs), lax.rem(s, hs)
            fresh = item + 1

            @pl.when(s < hs)
            def _():
                for copy in weight_copies(h):
                    copy.wait()

            @pl.when(s < steps)
            def _():
                with jax.named_scope("hidden"):
                    hidden(s)

            @pl.when((s >= BEHIND) & (s < steps + BEHIND))
            def _():
                with jax.named_scope("activate"):
                    activate(s - BEHIND)

            turn = lax.rem(s, hs * cn)
            c = lax.div(s, hs * cn)
            front_core = core == 0
            mark = lambda at, stage, to, when: pl.when((turn == at) & when & (to < chunks))(lambda: stage(to))
            mark(3, gather.pass_hi, c, (c == 0) & ~front_core)
            mark(5, gather.pass_lo, c, (c == 0) & ~front_core)
            total = hs * cn
            mark(total - 13, gather.start, c + 1, front_core)
            mark(total - 8, gather.start, c + 1, ~front_core)
            mark(total - 6, gather.pass_hi, c + 1, front_core)
            mark(total - 4, gather.pass_lo, c + 1, front_core)
            mark(total - 4, gather.pass_hi, c + 1, ~front_core)
            mark(total - 2, gather.pass_lo, c + 1, ~front_core)

            @pl.when((h == hs - 1) & (fresh < items))
            def _():
                with jax.named_scope("ready"):
                    ready(fresh)

            offset = BEHIND + 2
            begun = lax.div(s - offset, total) - 1
            since = lax.rem(s - offset, total)

            @pl.when((s >= total + offset) & (begun < chunks - 1))
            def _():
                @pl.when(since == 0)
                def _():
                    for f in range(cn):
                        with jax.named_scope("activated"):
                            activated(begun * cn + f)

                stretch(since, 0, 2, lambda i: down_all(begun, i))
                stretch(since, 2, 2, lambda i: within(i, add_core, begun * cn + core))
                stretch(since, 5, 2, lambda i: within(i, add_lo, begun * cn + core))

            for f in range(cn - 1):
                item = (chunks - 1) * cn + f
                opened = s - (hs * (item + 1) + BEHIND + 1)

                @pl.when(opened == 0)
                def _(item=item):
                    with jax.named_scope("activated"):
                        activated(item)

                stretch(opened, 0, 4, lambda i, item=item: down_one(item, i))
                stretch(opened, 1, 4, lambda i, item=item: owned(item, i, add_core))
                stretch(opened, 3, 4, lambda i, item=item: owned(item, i, add_lo))

            return carry

        lax.fori_loop(0, steps + BEHIND, step, 0)
        with jax.named_scope("activated_last"):
            activated(items - 1)

        def last(i, carry):
            down_one(items - 1, i)
            owned(items - 1, i - LAG, add_core)
            owned(items - 1, i - 2 * LAG - 1, add_lo)
            return carry

        lax.fori_loop(0, 2 * fs + LAG, last, 0)
        for c in range(chunks):

            def end(i, carry, c=c):
                within(i, add_hi, c * cn + core)
                return carry

            lax.fori_loop(0, fs, end, 0)

        def sent_rows(c, carry):
            gather.sent(c)
            return carry

        with jax.named_scope('sent_rows'):
            lax.fori_loop(0, chunks, sent_rows, 0)

        def sent_steps(s, carry):
            for d in range(1, kn):

                @pl.when(s >= steps - PARTS)
                def _(d=d):
                    part_copy(s, d).wait_send()

                act_copy(s, d).wait_send()
            return carry

        with jax.named_scope('sent_steps'):
            lax.fori_loop(0, steps, sent_steps, 0)

        for item in range(items):
            for i in range(fs):
                if item // cn * fs + i + t_slots >= chunks * fs:
                    each_core(item, lambda d, item=item, i=i: down_send(item, i, d).wait_send())

        def sent_pieces(j, carry):
            item, i = lax.div(j, fs) * cn + core, lax.rem(j, fs)
            for d in range(1, ln):
                mid_send(item, i, d).wait_send()
            for d in range(1, hn):
                low_send(item, i, d).wait_send()
            return carry

        with jax.named_scope('sent_pieces'):
            lax.fori_loop(0, chunks * fs, sent_pieces, 0)
        for t in range(1, n):
            block_copy(t).wait_send()
        for d in range(1, kn):

            def cross_sent(j, carry, d=d):
                cross_copy(d, origin(lax.rem(k + d, kn) * per + j)).wait_send()
                return carry

            lax.fori_loop(0, per, cross_sent, 0)
            square_copy(d).wait_send()

    b16 = jnp.bfloat16
    pl.run_scoped(
        attention_phase,
        pltpu.VMEM((heads, span, size), b16),
        pltpu.VMEM((heads, span, size), b16),
        pltpu.VMEM(wo_hbm.shape, b16),
        pltpu.VMEM((rows, span), jnp.float32),
        pltpu.VMEM((rows, nodes), jnp.float32),
        pltpu.VMEM((heads, rows, 2 * size), jnp.float32),
        pltpu.VMEM((heads, mine, wide), b16),
        pltpu.VMEM((n * mine, fb), jnp.float32),
    )
    pl.run_scoped(
        forward_phase,
        pltpu.VMEM((hs, width, 2 * hc), b16),
        pltpu.VMEM((3, hidden_width, fw), b16),
    )


def layer(
    queries, tree_keys, tree_values, keys, values, lengths, parents, residual, out_weight, norm_gain, gate_weight, up_weight,
    down_weight,
):
    dims = (*split_count(lax.axis_size("req")), lax.axis_size("ffn"))
    hn, ln, cn = dims
    kn = lax.axis_size("kvh")
    n = math.prod(dims)
    heads, span, size = keys.shape
    nodes, width = queries.shape
    wide = width // heads
    rows = wide // size * nodes
    mine, cols = residual.shape
    fb = out_weight.shape[1]
    hidden = gate_weight.shape[1]
    hc = lane_block(hidden, 256)
    fw = lane_block(cols, max(128, cols // 8))
    chunks = mine // ROWS
    items = chunks * cn
    tokens = n // cn * ROWS
    keep = tokens // kn
    steps = items * (hidden // hc)
    kept = chunks * (cols // fw)
    vmem = pl.BlockSpec(memory_space=pltpu.VMEM)
    hbm = pl.BlockSpec(memory_space=pl.ANY)
    f32, b16 = jnp.float32, jnp.bfloat16
    dma = pltpu.SemaphoreType.DMA
    return pl.pallas_call(
        functools.partial(layer_body, dims=dims, kn=kn, heads=heads, hc=hc, fw=fw),
        out_shape=jax.ShapeDtypeStruct(residual.shape, f32),
        in_specs=[
            pl.BlockSpec(memory_space=pltpu.SMEM), vmem, vmem, vmem, hbm, hbm, vmem, hbm, vmem, hbm, hbm, hbm, hbm,
        ],
        out_specs=vmem,
        scratch_shapes=[
            pltpu.VMEM((n * mine, width), b16),
            pltpu.VMEM((mine, cols), f32),
            pltpu.VMEM((mine, cols), b16),
            pltpu.VMEM((heads, cn - 1, rows // cn, 2 * size), f32),
            pltpu.VMEM((n * mine, fb), b16),
            pltpu.VMEM((n, mine, fb), b16),
            pltpu.VMEM((kn - 1, n, mine, fb), b16),
            pltpu.VMEM((mine, 128), f32),
            pltpu.VMEM((kn - 1, mine, 128), f32),
            pltpu.VMEM((BEHIND + 1, tokens, 2 * hc), f32),
            pltpu.VMEM((PARTS, kn - 1, keep, 2 * hc), b16),
            pltpu.VMEM((steps, kn - 1, keep, 2 * hc), b16),
            pltpu.VMEM((items, tokens, hidden), b16),
            pltpu.VMEM((cols // fw + 3, tokens, fw), f32),
            pltpu.VMEM((kept, cn - 1, tokens, fw), f32),
            pltpu.VMEM((kept, ln - 1, hn * ROWS, fw), b16),
            pltpu.VMEM((cols // fw, hn * ROWS, fw), f32),
            pltpu.VMEM((kept, ln - 1, hn * ROWS, fw), b16),
            pltpu.VMEM((kept, hn - 1, ROWS, fw), b16),
            pltpu.VMEM((kept, ROWS, fw), f32),
            pltpu.VMEM((kept, hn - 1, ROWS, fw), b16),
            dma((heads,)),
            dma((heads,)),
            dma,
            dma,
            dma((2, hidden // hc)),
            dma((3,)),
            *gather_sems(heads, dims),
            *gather_sems(chunks, dims),
            dma((heads, cn - 1)),
            dma((heads, cn - 1)),
            dma((n,)),
            dma((n,)),
            dma((kn - 1, n)),
            dma((kn - 1, n)),
            dma((kn - 1,)),
            dma((kn - 1,)),
            dma((steps, kn - 1)),
            dma((steps, kn - 1)),
            dma((steps, kn - 1)),
            dma((steps, kn - 1)),
            dma((cn - 1, kept)),
            dma((kept, cn - 1)),
            dma((kept, ln - 1)),
            dma((kept, ln - 1)),
            dma((kept, hn - 1)),
            dma((kept, hn - 1)),
        ],
        compiler_params=pltpu.CompilerParams(collective_id=1, has_side_effects=True, vmem_limit_bytes=63 * 1024 * 1024),
    )(
        lengths, queries, tree_keys, tree_values, keys, values, parents, residual, norm_gain[None, :], out_weight,
        gate_weight, up_weight, down_weight,
    )


def local(
    queries, tree_keys, tree_token_values, cache_keys, cached_value_rows, lengths, parents, residual, out_weight, norm_gain,
    gate_weight, up_weight, down_weight,
):
    return layer(
        queries[0], tree_keys[0], tree_token_values[0], cache_keys[0], cached_value_rows[0], lengths, parents, residual,
        out_weight, norm_gain, gate_weight, up_weight, down_weight,
    )


def solution(mesh):
    in_specs = (
        P("req", None, "kvh"),
        P("req", None, "kvh"),
        P("req", None, "kvh"),
        P("req", "kvh", "ffn", None),
        P("req", "kvh", "ffn", None),
        P(),
        P("req", None),
        P(("req", "ffn"), "kvh"),
        P("kvh", ("req", "ffn")),
        P("kvh"),
        P("kvh", ("req", "ffn")),
        P("kvh", ("req", "ffn")),
        P(("req", "ffn"), "kvh"),
    )
    out_specs = P(("req", "ffn"), "kvh")
    return jax.shard_map(local, mesh=mesh, in_specs=in_specs, out_specs=out_specs, check_vma=False)
```

```python
import functools
import math

import jax
import jax.numpy as jnp
from jax import lax
from jax.experimental import pallas as pl
from jax.experimental.pallas import tpu as pltpu
from jax.sharding import PartitionSpec as P

MASKED = -1e30
EPSILON = 1e-05
MESH = pl.DeviceIdType.MESH
ROWS = 16
LAG = 4
BEHIND = 4
PARTS = 8


def split_count(n):
    lo = math.isqrt(n)
    while n % lo:
        lo -= 1
    return n // lo, lo


def lane_block(width, most):
    return max(b for b in range(128, most + 1, 128) if width % b == 0)


def remote(src, dst, send, recv, where):
    return pltpu.make_async_remote_copy(
        src_ref=src, dst_ref=dst, send_sem=send, recv_sem=recv, device_id=where, device_id_type=MESH
    )


class Gather:
    def __init__(self, dims, line, source, target, sems):
        self.dims, self.line, self.source, self.target = dims, line, source, target
        self.z_send, self.z_recv, self.y_send, self.y_recv, self.c_send, self.c_recv, self.own_sem = sems
        req = lax.axis_index("req")
        self.hi, self.lo, self.core = req // dims[1], lax.rem(req, dims[1]), lax.axis_index("ffn")

    def place(self, c, o, g, f=None):
        hn, ln, cn = self.dims
        f = self.core if f is None else f
        return self.target(c, (f * ln + lax.rem(self.lo + ln - g, ln)) * hn + o, 1)

    def z_copy(self, c, o, up):
        step = 1 if up else -1
        where = {"req": (self.hi + step) * self.dims[1] + self.lo}
        spot = self.place(c, o, 0)
        return remote(spot, spot, self.z_send.at[c], self.z_recv.at[c, o], where)

    def z_own(self, c, up):
        step = 1 if up else -1
        where = {"req": (self.hi + step) * self.dims[1] + self.lo}
        o = self.hi
        return remote(
            self.source(c), self.place(c, o, 0), self.z_send.at[c], self.z_recv.at[c, o], where
        )

    def z_far(self, c, e, up):
        o = self.hi
        where = {"req": (o + (e if up else -e)) * self.dims[1] + self.lo}
        return remote(self.source(c), self.place(c, o, 0), self.z_send.at[c], self.z_recv.at[c, o], where)

    def far(self, body):
        for e in range(1, self.dims[0]):

            def above(e=e):
                @pl.when(self.hi + e < self.dims[0])
                def _():
                    body(e, True)

            def below(e=e):
                @pl.when(self.hi >= e)
                def _():
                    body(e, False)

            self.end_first(below, above)

    def y_copy(self, c, o, d, own=False):
        ln = self.dims[1]
        where = {"req": self.hi * ln + lax.rem(self.lo + d, ln)}
        src = self.source(c) if own else self.place(c, o, 0)
        return remote(src, self.place(c, o, 0), self.y_send.at[c], self.y_recv.at[c, o, d - 1], where)

    def c_copy(self, c, o, g, d, own=False):
        where = {"ffn": lax.rem(self.core + d, self.dims[2])}
        src = self.source(c) if own else self.place(c, o, g)
        return remote(src, self.place(c, o, g), self.c_send.at[c], self.c_recv.at[c, g, d - 1], where)

    def own_copy(self, c):
        return pltpu.make_async_copy(self.source(c), self.place(c, self.hi, 0), self.own_sem.at[c])

    def end_first(self, down, up):
        low = 2 * self.hi < self.dims[0]
        for first in (True, False):

            @pl.when(low if first else ~low)
            def _(first=first):
                for stage in (down, up) if first else (up, down):
                    stage()

    def around(self, e, body):
        def below():
            @pl.when(self.hi >= e)
            def _():
                body(self.hi - e, True)

        def above():
            @pl.when(self.hi + e < self.dims[0])
            def _():
                body(self.hi + e, False)

        self.end_first(above, below)

    def onward(self, up, body):
        @pl.when(self.hi + 1 < self.dims[0] if up else self.hi > 0)
        def _():
            body()

    def start(self, c):
        self.start_hi(c)
        self.start_rest(c)

    def start_hi(self, c):
        if self.line:
            self.end_first(*(lambda up=up: self.onward(up, lambda: self.z_own(c, up).start()) for up in (False, True)))
        else:
            self.far(lambda e, up: self.z_far(c, e, up).start())

    def start_rest(self, c):
        hn, ln, cn = self.dims
        for d in range(1, ln):
            self.y_copy(c, self.hi, d, True).start()
        for d in range(1, cn):
            self.c_copy(c, self.hi, 0, d, True).start()
        self.own_copy(c).start()

    def pass_hi(self, c, reach=None):
        hn, ln, cn = self.dims

        def one(o, up):
            self.z_copy(c, o, up).wait_recv()
            if self.line:
                self.onward(up, lambda: self.z_copy(c, o, up).start())
            for d in range(1, ln):
                self.y_copy(c, o, d).start()
            for d in range(1, cn):
                self.c_copy(c, o, 0, d).start()

        for e in range(1, hn) if reach is None else [reach]:
            self.around(e, one)

    def pass_lo(self, c):
        hn, ln, cn = self.dims

        def one(o, up):
            for g in range(1, ln):
                self.y_copy(c, o, g).wait_recv()
                for d in range(1, cn):
                    self.c_copy(c, o, g, d).start()

        one(self.hi, True)
        for e in range(1, hn):
            self.around(e, one)

    def take(self, c, d, parts=None):
        hn, ln, cn = self.dims
        where = {"ffn": lax.rem(self.core + d, cn)}
        for g in range(ln) if parts is None else parts:
            f, b = lax.rem(self.core + cn - d, cn), lax.rem(self.lo + ln - g, ln)
            spot = self.target(c, (f * ln + b) * hn, hn)
            remote(spot, spot, self.c_send.at[c], self.c_recv.at[c, g, d - 1], where).wait_recv()

    def sent(self, c):
        hn, ln, cn = self.dims
        where = {"ffn": lax.rem(self.core + 1, cn)}

        def gone(sem, count):
            spot = self.target(c, 0, count)
            remote(spot, spot, sem.at[c], self.c_recv.at[c, 0, 0], where).wait_send()

        if self.line:
            inner = (self.hi > 0) & (self.hi + 1 < hn)
            pl.when(inner)(lambda: gone(self.z_send, hn + 1))
            pl.when(~inner)(lambda: gone(self.z_send, 1))
        else:
            gone(self.z_send, hn - 1)
        gone(self.y_send, hn * (ln - 1))
        gone(self.c_send, hn * ln * (cn - 1))


def gather_sems(count, dims):
    hn, ln, cn = dims
    dma = pltpu.SemaphoreType.DMA
    return [
        dma((count,)),
        dma((count, hn)),
        dma((count,)),
        dma((count, hn, ln - 1)),
        dma((count,)),
        dma((count, ln, cn - 1)),
        dma((count,)),
    ]


def layer_body(
    len_ref, q_ref, tk_ref, tv_ref, k_hbm, v_hbm, par_ref, res_hbm, gain_ref, wo_hbm, gate_hbm, up_hbm, down_hbm, out_ref,
    gath, state, normed, half_got, pack, pack_got, red, blocks_got, cross_got, squares, squares_got, line_own, lines, factor_of,
    rbuf, part, got, act, dbuf, got_core, mid, own_mid, got_lo, low, own_low, got_hi,
    k_sem, v_sem, wo_sem, res_sem, w_sem, wd_sem,
    a0, a1, a2, a3, a4, a5, a6, d0, d1, d2, d3, d4, d5, d6,
    x_send, x_recv, y_send, y_recv, b_send, b_recv, f_send, f_recv, s_send, s_recv, r_send, r_recv, told,
    p_send, p_recv, a_send, a_recv, c_send, c_recv, l_send, l_recv, h_send, h_recv,
    *, dims, kn, heads, hc, fw,
):
    hn, ln, cn = dims
    n = hn * ln * cn
    req = lax.axis_index("req")
    hi, lo, core, k = req // ln, lax.rem(req, ln), lax.axis_index("ffn"), lax.axis_index("kvh")
    span, size = k_hbm.shape[1:]
    nodes = q_ref.shape[0]
    group = q_ref.shape[1] // (heads * size)
    wide = group * size
    rows = group * nodes
    mine = nodes // cn
    part_rows = group * mine
    fb = red.shape[2]
    per = n // kn
    width = normed.shape[1]
    features = width * kn
    factor = size**-0.5 * math.log2(math.e)
    chunk = math.gcd(span, 1024)
    hidden_width = act.shape[2]
    hs = hidden_width // hc
    fs = width // fw
    to_hi = lambda d: {"req": lax.rem(hi + d, hn) * ln + lo}
    to_lo = lambda d: {"req": hi * ln + lax.rem(lo + d, ln)}
    to_core = lambda d: {"ffn": lax.rem(core + d, cn)}
    to_kvh = lambda d: {"kvh": lax.rem(k + d, kn)}
    flat = [(e, g, d) for e in range(hn) for g in range(ln) for d in range(cn)]

    def plane(e, g, d):
        return {"req": lax.rem(hi + e, hn) * ln + lax.rem(lo + g, ln), "ffn": lax.rem(core + d, cn)}

    own_block = (core * ln + lo) * hn + hi
    barrier = pltpu.get_barrier_semaphore()
    peers = [plane(*t) for t in flat[1:]] + [to_kvh(d) for d in range(1, kn)]
    for where in peers:
        pl.semaphore_signal(barrier, inc=1, device_id=where, device_id_type=MESH)

    def attention_phase(kbuf, vbuf, wo, sbuf, tree_mask, half_own, attn, proj):
        k_copy = lambda h: pltpu.make_async_copy(k_hbm.at[h], kbuf.at[h], k_sem.at[h])
        v_copy = lambda h: pltpu.make_async_copy(v_hbm.at[h], vbuf.at[h], v_sem.at[h])
        wo_copy = pltpu.make_async_copy(wo_hbm, wo, wo_sem)
        for h in range(heads):
            k_copy(h).start()
            v_copy(h).start()
        wo_copy.start()
        pltpu.make_async_copy(res_hbm, state, res_sem).start()
        live = jnp.clip(len_ref[lax.axis_index("req")] - core * span, 0, span)

        up = lax.broadcasted_iota(jnp.int32, (nodes, nodes), 0)
        across = lax.broadcasted_iota(jnp.int32, (nodes, nodes), 1)
        eye = jnp.where(up == across, 1.0, 0.0).astype(jnp.bfloat16)
        link = jnp.where(up == par_ref[...], 1.0, 0.0).astype(jnp.bfloat16)
        over = lax.dot_general(link, eye, (((0,), (0,)), ((), ())), preferred_element_type=jnp.float32)
        reach = jnp.minimum(over + jnp.where(up == across, 1.0, 0.0), 1.0)
        for _ in range((nodes - 1).bit_length()):
            half = reach.astype(jnp.bfloat16)
            reach = jnp.minimum(jnp.dot(half, half, preferred_element_type=jnp.float32), 1.0)
        reach = reach * jnp.where(core == 0, 1.0, 0.0)
        tree_mask[...] = jnp.concatenate(
            [reach[f * mine : (f + 1) * mine] for f in range(cn) for _ in range(group)], axis=0
        )
        def head_cols(h):
            return pl.ds(pl.multiple_of(h * size, size), size)

        def queries_of(h):
            return jnp.concatenate(
                [
                    q_ref[f * mine : (f + 1) * mine, pl.ds(pl.multiple_of((h * group + g) * size, size), size)]
                    for f in range(cn)
                    for g in range(group)
                ],
                axis=0,
            )

        def tree_scores(h):
            s = lax.dot_general(
                queries_of(h), tk_ref[:, head_cols(h)], (((1,), (1,)), ((), ())), preferred_element_type=jnp.float32
            )
            return jnp.where(tree_mask[...] > 0.5, s, MASKED)

        def score(h):
            k_copy(h).wait()
            q = queries_of(h)
            first = kbuf[h, pl.ds(0, 16), :].astype(jnp.float32)[0:1]
            top = jnp.max(tree_scores(h), axis=1, keepdims=True)
            for c in range(span // chunk):
                spot = c * chunk + lax.broadcasted_iota(jnp.int32, (chunk, size), 0)
                keys = jnp.where(spot < live, kbuf[h, pl.ds(c * chunk, chunk), :].astype(jnp.float32), first)
                s = lax.dot_general(
                    q, keys.astype(jnp.bfloat16), (((1,), (1,)), ((), ())), preferred_element_type=jnp.float32
                )
                sbuf[:, pl.ds(c * chunk, chunk)] = s
                top = jnp.maximum(top, jnp.max(s, axis=1, keepdims=True))
            half_own[h, :, pl.ds(size, size)] = jnp.broadcast_to(top, (rows, size))

        def weigh(h):
            v_copy(h).wait()
            top = half_own[h, :, pl.ds(size, 1)]
            usable = tree_mask[...] > 0.5
            w = jnp.where(usable, jnp.exp2((tree_scores(h) - top) * factor), 0.0).astype(jnp.bfloat16)
            ones = jnp.ones((nodes, size), jnp.bfloat16)
            total = jnp.dot(
                w, jnp.concatenate([tv_ref[:, head_cols(h)], ones], axis=1), preferred_element_type=jnp.float32
            )
            for c in range(span // chunk):
                spot = c * chunk + lax.broadcasted_iota(jnp.int32, (chunk, size), 0)
                usable = spot < live
                values = jnp.where(usable, vbuf[h, pl.ds(c * chunk, chunk), :].astype(jnp.float32), 0.0)
                count = jnp.where(usable, 1.0, 0.0)
                both = jnp.concatenate([values.astype(jnp.bfloat16), count.astype(jnp.bfloat16)], axis=1)
                w = jnp.exp2((sbuf[:, pl.ds(c * chunk, chunk)] - top) * factor).astype(jnp.bfloat16)
                total = total + jnp.dot(w, both, preferred_element_type=jnp.float32)
            seen = jnp.where((live > 0) | (core == 0), 1.0, 0.0)
            top = jnp.where(seen > 0.5, top * factor, MASKED)
            lane = lax.broadcasted_iota(jnp.int32, (rows, size), 1)
            half_own[h, :, pl.ds(0, size)] = total[:, :size]
            half_own[h, :, pl.ds(size, size)] = jnp.where(lane < size // 2, total[:, size:], top)
            for d in range(1, cn):
                half_copy(h, d).start()
        def part_of(f):
            return pl.ds(pl.multiple_of(f * part_rows, part_rows), part_rows)

        def half_copy(h, d):
            src = half_own.at[h, part_of(lax.rem(core + d, cn)), :]
            return remote(src, half_got.at[h, d - 1], x_send.at[d - 1], x_recv.at[h, d - 1], to_core(d))

        def merge(h):
            for d in range(1, cn):
                half_copy(h, d).wait_recv()
            pieces = [half_own[h, part_of(core), :]] + [half_got[h, d] for d in range(cn - 1)]
            tops = [p[:, size + size // 2 : size + size // 2 + 1] for p in pieces]
            best = functools.reduce(jnp.maximum, tops)
            above, below = 0.0, 0.0
            for p, t in zip(pieces, tops):
                scale = jnp.exp2(t - best)
                above = above + p[:, :size] * scale
                below = below + p[:, size : size + 1] * scale
            result = (above / below).astype(jnp.bfloat16)
            for g in range(group):
                attn[h, :, pl.ds(g * size, size)] = result[g * mine : (g + 1) * mine]
        gather = Gather(
            dims,
            True,
            lambda h: attn.at[h],
            lambda h, b, count: gath.at[
                pl.ds(pl.multiple_of(b * mine, mine), count * mine), pl.ds(pl.multiple_of(h * wide, wide), wide)
            ],
            (a0, a1, a2, a3, a4, a5, a6),
        )

        def finish(h):
            for d in range(1, cn):
                gather.take(h, d)
            gather.own_copy(h).wait()

        def project(h):
            cols = pl.ds(pl.multiple_of(h * wide, wide), wide)
            piece = jnp.dot(gath[:, cols], wo[cols, :], preferred_element_type=jnp.float32)

            @pl.when(h == 0)
            def _():
                proj[...] = piece

            @pl.when(h > 0)
            def _():
                proj[...] = proj[...] + piece

        def guarded(h, *stages):
            @pl.when((h >= 0) & (h < heads))
            def _():
                for stage in stages:
                    with jax.named_scope(stage.__name__):
                        stage(h)

        def step(i, carry):
            guarded(i, score)

            @pl.when(i == 0)
            def _():
                with jax.named_scope("barrier_wait"):
                    pl.semaphore_wait(barrier, len(peers))

            guarded(i - 1, merge, gather.start)
            for e in range(1, hn):

                def pass_hi(h, e=e):
                    gather.pass_hi(h, e)

                guarded(i - 1 - e, pass_hi)
            guarded(i, weigh)
            guarded(i - 1 - hn, gather.pass_lo)

            @pl.when(i == 2)
            def _():
                wo_copy.wait()

            guarded(i - 2 - hn, finish, project)
            return carry

        lax.fori_loop(0, heads + 2 + hn, step, 0)
        def sent(h, carry):
            gather.sent(h)
            return carry

        lax.fori_loop(0, heads, sent, 0)
        for d in range(1, cn):
            spot = half_got.at[:, d - 1]
            remote(spot, spot, x_send.at[d - 1], x_recv.at[0, d - 1], to_core(d)).wait_send()

        def rows_of(b):
            return pl.ds(pl.multiple_of(b * mine, mine), mine)

        def halve_copy(m, d):
            return remote(pack.at[d - 1, m], pack_got.at[d - 1, m], y_send.at[d - 1], y_recv.at[d - 1, m], to_kvh(d))

        order = sorted(range(hn), key=lambda e: -min(e, hn - e))

        def in_order(i):
            e, q = lax.div(i, per // hn), lax.rem(i, per // hn)
            shift = functools.reduce(lambda x, at: jnp.where(e == at, order[at], x), range(hn), 0)
            return q * hn + lax.rem(hi + shift, hn)

        def halve(i, carry):
            m = in_order(i)
            for d in range(1, kn):
                pack[d - 1, m] = proj[rows_of(lax.rem(k + d, kn) * per + m), :].astype(jnp.bfloat16)
                halve_copy(m, d).start()
            return carry

        lax.fori_loop(0, per, halve, 0)

        def deliver(i, carry):
            m = in_order(i)
            b = k * per + m
            total = proj[rows_of(b), :]
            for d in range(1, kn):
                halve_copy(m, d).wait_recv()
                total = total + pack_got[d - 1, m].astype(jnp.float32)
            red[m] = total.astype(jnp.bfloat16)
            own = req * cn + core

            @pl.when(b == own_block)
            def _():
                blocks_got[own] = red[m]

            @pl.when(b != own_block)
            def _():
                f, r = lax.div(b, ln * hn), lax.rem(b, ln * hn)
                where = {"req": lax.rem(r, hn) * ln + lax.div(r, hn), "ffn": f}
                remote(red.at[m], blocks_got.at[own], b_send, b_recv.at[own], where).start()

            return carry

        with jax.named_scope("deliver"):
            lax.fori_loop(0, per, deliver, 0)

    def forward_phase(wgu, wd):
        wd_slots, r_slots, m_slots, t_slots = wd.shape[0], rbuf.shape[0], own_mid.shape[0], dbuf.shape[0] - fs
        chunks = mine // ROWS
        items = chunks * cn
        steps = items * hs
        loads = (chunks - 2 + cn) * fs + wd_slots
        tokens = n // cn * ROWS
        keep = tokens // kn
        half_rows = hn * ROWS

        def weight_copies(h):
            cols = pl.ds(pl.multiple_of(h * hc, hc), hc)
            return (
                pltpu.make_async_copy(gate_hbm.at[:, cols], wgu.at[h, :, pl.ds(0, hc)], w_sem.at[h]),
                pltpu.make_async_copy(up_hbm.at[:, cols], wgu.at[h, :, pl.ds(hc, hc)], w_sem.at[h]),
            )

        def down_copy(j):
            slot = lax.rem(j, wd_slots)
            cols = pl.ds(pl.multiple_of(lax.rem(j, fs) * fw, fw), fw)
            return pltpu.make_async_copy(down_hbm.at[:, cols], wd.at[slot], wd_sem.at[slot])

        for h in range(hs):
            for copy in weight_copies(h):
                copy.start()
        for j in range(min(wd_slots, loads)):
            down_copy(j).start()
        kept_here = lax.div(own_block, per) == k
        keeper = lax.div(own_block, per)

        def cross_copy(j, d):
            b = lax.rem(k + d, kn) * per + j
            return remote(blocks_got.at[b], cross_got.at[j], f_send.at[d - 1], f_recv.at[j], to_kvh(d))

        def arrived(b):
            @pl.when(b != req * cn + core)
            def _():
                remote(red.at[0], blocks_got.at[b], b_send, b_recv.at[b], to_core(1)).wait_recv()

        @pl.when(kept_here)
        def _():
            for d in range(1, kn):

                def forward(j, carry, d=d):
                    arrived(lax.rem(k + d, kn) * per + j)
                    cross_copy(j, d).start()
                    return carry

                lax.fori_loop(0, per, forward, 0)

        def collect(j, square):
            cols = pl.ds(pl.multiple_of(j * fb, fb), fb)

            @pl.when(kept_here)
            def _():
                arrived(k * per + j)
                state[:, cols] = state[:, cols] + blocks_got[k * per + j].astype(jnp.float32)

            @pl.when(~kept_here)
            def _():
                cross_copy(j, 1).wait_recv()
                state[:, cols] = state[:, cols] + cross_got[j].astype(jnp.float32)

            total = state[:, cols]
            normed[:, cols] = (total * gain_ref[:, cols]).astype(jnp.bfloat16)
            return square + jnp.sum(total * total, axis=1, keepdims=True)

        pltpu.make_async_copy(res_hbm, state, res_sem).wait()
        with jax.named_scope("collect"):
            square = lax.fori_loop(0, per, collect, jnp.zeros((mine, 1), jnp.float32))
        @pl.when(kept_here)
        def _():
            for d in range(1, kn):
                pl.semaphore_signal(told, inc=1, device_id=to_kvh(d), device_id_type=MESH)

        squares[...] = jnp.broadcast_to(square, squares.shape)

        def square_copy(d):
            return remote(squares, squares_got.at[d - 1], s_send.at[d - 1], s_recv.at[d - 1], to_kvh(d))

        for d in range(1, kn):
            square_copy(d).start()

        @pl.when(~kept_here)
        def _():
            pl.semaphore_wait(told, 1)

        def share_squares():
            total = squares[...]
            for d in range(1, kn):
                square_copy(d).wait_recv()
                total = total + squares_got[d - 1]
            same = lax.broadcasted_iota(jnp.int32, total.shape, 0) == lax.broadcasted_iota(jnp.int32, total.shape, 1)
            line = jnp.sum(jnp.where(same, total, 0.0), axis=0, keepdims=True)
            line_own[...] = jnp.broadcast_to(line, line_own.shape)
            lines[own_block] = line_own[...]
            for t in range(1, n):
                line_copy(t).start()

        def line_copy(t):
            return remote(line_own, lines.at[own_block], r_send, r_recv, plane(*flat[t]))

        def all_lines():
            return remote(lines.at[pl.ds(0, n - 1)], lines.at[pl.ds(0, n - 1)], r_send, r_recv, plane(*flat[1]))

        def factors():
            all_lines().wait_recv()
            for item in range(items):
                for m in range(keep // ROWS):
                    b = (item % cn) * (ln * hn) + k * (keep // ROWS) + m
                    wide_line = jnp.broadcast_to(lines[b, pl.ds(0, 1), :], (ROWS, 128))
                    spot = lax.broadcasted_iota(jnp.int32, (ROWS, 128), 0) + (item // cn) * ROWS
                    picked = jnp.where(lax.broadcasted_iota(jnp.int32, (ROWS, 128), 1) == spot, wide_line, 0.0)
                    total = jnp.sum(picked, axis=1, keepdims=True)
                    column = lax.rsqrt(total / features + EPSILON)
                    factor_of[item, pl.ds(m * ROWS, ROWS), :] = jnp.broadcast_to(column, (ROWS, 128))
        gather = Gather(
            dims,
            False,
            lambda c: normed.at[pl.ds(pl.multiple_of(c * ROWS, ROWS), ROWS), :],
            lambda c, b, count: gath.at[pl.ds(pl.multiple_of(c * (n * ROWS) + b * ROWS, ROWS), count * ROWS), :],
            (d0, d1, d2, d3, d4, d5, d6),
        )

        def mine_of(item):
            return core == lax.rem(item, cn)

        def on_owner(item, stage):
            @pl.when(mine_of(item))
            def _():
                stage(lax.div(item, cn))

        def ready(item, own=True, parts=None):
            c = lax.div(item, cn)
            if own:

                @pl.when(mine_of(item))
                def _():
                    gather.own_copy(c).wait()

            for d in range(1, cn):

                @pl.when(lax.rem(core + cn - d, cn) == lax.rem(item, cn))
                def _(d=d):
                    gather.take(c, d, parts)

        item_rows = lambda item: pl.ds(pl.multiple_of(item * tokens, tokens), tokens)
        mine_rows = pl.ds(pl.multiple_of(k * keep, keep), keep)

        def part_copy(s, d):
            return remote(
                part.at[lax.rem(s, PARTS), d - 1], got.at[s, d - 1], p_send.at[lax.rem(s, PARTS), d - 1],
                p_recv.at[lax.rem(s, 3 * BEHIND), d - 1], to_kvh(d),
            )

        def hidden(s):
            item, h = lax.div(s, hs), lax.rem(s, hs)
            slot = lax.rem(s, r_slots)
            rbuf[slot] = jnp.dot(gath[item_rows(item), :], wgu[h], preferred_element_type=jnp.float32)
            for d in range(1, kn):

                @pl.when(s >= PARTS)
                def _(d=d):
                    part_copy(s - PARTS, d).wait_send()

                theirs = pl.ds(pl.multiple_of(lax.rem(k + d, kn) * keep, keep), keep)
                part[lax.rem(s, PARTS), d - 1] = rbuf[slot, theirs, :].astype(jnp.bfloat16)
                part_copy(s, d).start()

        def act_copy(s, d):
            item, h = lax.div(s, hs), lax.rem(s, hs)
            spot = act.at[item, mine_rows, pl.ds(pl.multiple_of(h * hc, hc), hc)]
            return remote(spot, spot, a_send.at[d - 1], a_recv.at[item, d - 1], to_kvh(d))

        def activate(s):
            item, h = lax.div(s, hs), lax.rem(s, hs)
            slot = lax.rem(s, r_slots)
            for d in range(1, kn):
                part_copy(s, d).wait_recv()
            gate = rbuf[slot, mine_rows, pl.ds(0, hc)]
            up = rbuf[slot, mine_rows, pl.ds(hc, hc)]
            for d in range(kn - 1):
                gate = gate + got[s, d, :, pl.ds(0, hc)].astype(jnp.float32)
                up = up + got[s, d, :, pl.ds(hc, hc)].astype(jnp.float32)
            scale = factor_of[item, :, pl.ds(0, 1)]
            gate, up = gate * scale, up * scale
            value = (gate / (1.0 + jnp.exp(-gate)) * up).astype(jnp.bfloat16)
            act[item, mine_rows, pl.ds(pl.multiple_of(h * hc, hc), hc)] = value
            for d in range(1, kn):
                act_copy(s, d).start()

        def activated(item):
            for d in range(1, kn):
                theirs = pl.ds(pl.multiple_of(lax.rem(k + kn - d, kn) * keep, keep), keep)
                spot = act.at[item, theirs, :]
                remote(spot, spot, a_send.at[d - 1], a_recv.at[item, d - 1], to_kvh(d)).wait_recv()

        def kept(item, i):
            return lax.div(item, cn) * fs + i

        def down_slot(item, i):
            j = kept(item, i)
            return jnp.where(mine_of(item), lax.rem(j, fs), fs + lax.rem(j, t_slots))

        def down_send(item, i, d):
            j = kept(item, i)
            return remote(
                dbuf.at[fs + lax.rem(j, t_slots)], got_core.at[j, d - 1], c_send.at[d - 1, lax.rem(j, t_slots)],
                c_recv.at[j, d - 1], to_core(d),
            )

        def each_core(item, body):
            for d in range(1, cn):

                @pl.when(lax.rem(core + d, cn) == lax.rem(item, cn))
                def _(d=d):
                    body(d)

        spare = min(fs - wd_slots, hs)

        def spare_copy(i):
            cols = pl.ds((wd_slots + i) * fw, fw)
            room = wgu.at[i, pl.ds(0, hidden_width), pl.ds(0, fw)]
            return pltpu.make_async_copy(down_hbm.at[:, cols], room, w_sem.at[i])

        def settle(members, i, result):
            for at, item in enumerate(members):

                @pl.when(kept(item, i) >= t_slots)
                def _(item=item):
                    each_core(item, lambda d: down_send(item, i - t_slots, d).wait_send())

                dbuf[down_slot(item, i)] = result[at * tokens : (at + 1) * tokens]
                each_core(item, lambda d, item=item: down_send(item, i, d).start())

        def multiply(load, members, i):
            down_copy(load).wait()
            first = members[0]
            rows = act[pl.ds(first, len(members))].reshape(len(members) * tokens, hidden_width)
            settle(members, i, jnp.dot(rows, wd[lax.rem(load, wd_slots)], preferred_element_type=jnp.float32))

            @pl.when(load + wd_slots < loads)
            def _():
                down_copy(load + wd_slots).start()

        def multiply_spare(item, i):
            pltpu.make_async_copy(
                down_hbm.at[:, pl.ds(0, fw)], wgu.at[0, pl.ds(0, hidden_width), pl.ds(0, fw)], w_sem.at[i - wd_slots]
            ).wait()
            weight = wgu[i - wd_slots, pl.ds(0, hidden_width), pl.ds(0, fw)]
            settle([item], i, jnp.dot(act[item], weight, preferred_element_type=jnp.float32))

        def mid_send(item, i, d):
            j = kept(item, i)
            return remote(mid.at[j, d - 1], got_lo.at[j, d - 1], l_send.at[d - 1], l_recv.at[j, d - 1], to_lo(d))

        def low_send(item, i, d):
            j = kept(item, i)
            return remote(low.at[j, d - 1], got_hi.at[j, d - 1], h_send, h_recv.at[j], to_hi(d))

        def add_core(item, i):
            j = kept(item, i)
            slot = lax.rem(j, fs)
            for d in range(1, cn):
                down_send(item, i, d).wait_recv()

            def total(b):
                at = pl.ds(pl.multiple_of(b * half_rows, half_rows), half_rows)
                result = dbuf[slot, at, :]
                for d in range(cn - 1):
                    result = result + got_core[j, d, at, :]
                return result

            for d in range(1, ln):
                mid[j, d - 1] = total(lax.rem(lo + d, ln)).astype(jnp.bfloat16)
                mid_send(item, i, d).start()
            own_mid[lax.rem(j, m_slots)] = total(lo)

        def add_lo(item, i):
            j = kept(item, i)
            slot = lax.rem(j, m_slots)
            for d in range(1, ln):
                mid_send(item, i, d).wait_recv()

            def total(h):
                at = pl.ds(pl.multiple_of(h * ROWS, ROWS), ROWS)
                result = own_mid[slot, at, :]
                for d in range(ln - 1):
                    result = result + got_lo[j, d, at, :].astype(jnp.float32)
                return result

            for d in range(1, hn):
                low[j, d - 1] = total(lax.rem(hi + d, hn)).astype(jnp.bfloat16)
                low_send(item, i, d).start()
            own_low[j] = total(hi)

        def add_hi(item, i):
            j = kept(item, i)
            c = lax.div(item, cn)
            remote(got_hi.at[j], got_hi.at[j], h_send, h_recv.at[j], to_hi(1)).wait_recv()
            result = own_low[j]
            for d in range(hn - 1):
                result = result + got_hi[j, d].astype(jnp.float32)
            at = (pl.ds(pl.multiple_of(c * ROWS, ROWS), ROWS), pl.ds(pl.multiple_of(i * fw, fw), fw))
            out_ref[at] = state[at] + result

        def within(i, stage, *args):
            @pl.when((i >= 0) & (i < fs))
            def _():
                with jax.named_scope(stage.__name__.strip('<>')):
                    stage(*args, i)

        quick = -(-fs // 2)

        def down_all(c, i):
            within(i, lambda i: multiply(c * fs + i, [c * cn + f for f in range(cn)], i))

        def down_one(item, i):
            within(i, lambda i: multiply((chunks - 1 + item % cn) * fs + i, [item], i))

        def down_last(i):
            @pl.when(i < wd_slots)
            def _():
                multiply(loads - wd_slots + i, [items - 1], i)

            @pl.when((i >= wd_slots) & (i < fs))
            def _():
                multiply_spare(items - 1, i)

        def owned(item, i, stage):
            @pl.when(mine_of(item))
            def _():
                within(i, stage, item)

        def stretch(at, first, per_step, stage):
            @pl.when((at >= first) & (at - first < -(-fs // per_step)))
            def _():
                def one(i, carry):
                    stage((at - first) * per_step + i)
                    return carry

                lax.fori_loop(0, per_step, one, 0)

        on_owner(0, gather.start)
        pl.when((core > 0) & kept_here)(lambda: gather.start(0))
        with jax.named_scope("first_hi"):
            on_owner(0, gather.pass_hi)
            pl.when((core > 0) & kept_here)(lambda: gather.pass_hi(0))
        with jax.named_scope("share"):
            share_squares()
        with jax.named_scope("first_lo"):
            on_owner(0, gather.pass_lo)
        with jax.named_scope("first_ready"):
            ready(0, False, range(1))
            for f in range(1, cn):
                pl.when((core == f) & ~kept_here)(lambda: gather.start_hi(0))
            ready(0, True, range(1, ln))
            for f in range(1, cn):
                pl.when((core == f) & ~kept_here)(lambda: gather.start_rest(0))

        def step(s, carry):
            item, h = lax.div(s, hs), lax.rem(s, hs)
            fresh = item + 1

            @pl.when(s < hs)
            def _():
                pltpu.make_async_copy(gate_hbm.at[:, pl.ds(0, 2 * hc)], wgu.at[h], w_sem.at[h]).wait()

            @pl.when(s < steps)
            def _():
                with jax.named_scope("hidden"):
                    hidden(s)

            @pl.when((s >= BEHIND) & (s < steps + BEHIND))
            def _():
                @pl.when(s == BEHIND)
                def _():
                    with jax.named_scope("factors"):
                        factors()

                with jax.named_scope("activate"):
                    activate(s - BEHIND)

            turn = lax.rem(s, hs * cn)
            c = lax.div(s, hs * cn)
            front_core = core == 0
            mark = lambda at, stage, to, when: pl.when((turn == at) & when & (to < chunks))(lambda: stage(to))
            mark(1, gather.pass_lo, c, (c == 0) & ~front_core & kept_here)
            mark(3, gather.pass_hi, c, (c == 0) & ~front_core & ~kept_here)
            mark(5, gather.pass_lo, c, (c == 0) & ~front_core & ~kept_here)
            total = hs * cn
            mark(total - 13, gather.start, c + 1, front_core)
            mark(total - 8, gather.start, c + 1, ~front_core)
            mark(total - 6, gather.pass_hi, c + 1, front_core)
            mark(total - 4, gather.pass_lo, c + 1, front_core)
            mark(total - 4, gather.pass_hi, c + 1, ~front_core)
            mark(total - 2, gather.pass_lo, c + 1, ~front_core)

            @pl.when((h == hs - 1) & (fresh < items))
            def _():
                with jax.named_scope("ready"):
                    ready(fresh)

            offset = BEHIND + 3
            begun = lax.div(s - offset, total) - 1
            since = lax.rem(s - offset, total)

            @pl.when((s >= total + offset) & (begun < chunks - 1))
            def _():
                @pl.when(since == 0)
                def _():
                    for f in range(cn):
                        with jax.named_scope("activated"):
                            activated(begun * cn + f)

                stretch(since, 0, 2, lambda i: down_all(begun, i))
                stretch(since, 2, 2, lambda i: within(i, add_core, begun * cn + core))
                stretch(since, 5, 2, lambda i: within(i, add_lo, begun * cn + core))

            for f in range(cn - 1):
                item = (chunks - 1) * cn + f
                opened = s - (hs * (item + 1) + BEHIND + 2)

                @pl.when(opened == 0)
                def _(item=item):
                    with jax.named_scope("activated"):
                        activated(item)

                stretch(opened, 1, quick, lambda i, item=item: owned(item, i, add_core))
                stretch(opened, 0, quick, lambda i, item=item: down_one(item, i))

                if f == cn - 2:

                    @pl.when(opened == 1)
                    def _():
                        for i in range(spare):
                            spare_copy(i).start()


            return carry

        lax.fori_loop(0, steps + BEHIND, step, 0)
        with jax.named_scope("activated_last"):
            activated(items - 1)

        def last(i, carry):
            down_last(i)
            owned(items - 1, i - LAG, add_core)
            for f in range(cn - 1):
                owned((chunks - 1) * cn + f, i - LAG, add_lo)
            owned(items - 1, i - 2 * LAG - 1, add_lo)
            return carry

        lax.fori_loop(0, 2 * fs + LAG, last, 0)
        for c in range(chunks):

            def end(i, carry, c=c):
                within(i, add_hi, c * cn + core)
                return carry

            lax.fori_loop(0, fs, end, 0)

        def sent_rows(c, carry):
            gather.sent(c)
            return carry

        with jax.named_scope('sent_rows'):
            lax.fori_loop(0, chunks, sent_rows, 0)

        def sent_steps(s, carry):
            for d in range(1, kn):

                @pl.when(s >= steps - PARTS)
                def _(d=d):
                    part_copy(s, d).wait_send()

            return carry

        for d in range(1, kn):
            spot = act.at[:, mine_rows, :]
            remote(spot, spot, a_send.at[d - 1], a_recv.at[0, d - 1], to_kvh(d)).wait_send()
        with jax.named_scope('sent_steps'):
            lax.fori_loop(0, steps, sent_steps, 0)

        for item in range(items):
            for i in range(fs):
                if item // cn * fs + i + t_slots >= chunks * fs:
                    each_core(item, lambda d, item=item, i=i: down_send(item, i, d).wait_send())

        for d in range(1, ln):
            spot = mid.at[:, d - 1]
            remote(spot, spot, l_send.at[d - 1], l_recv.at[0, d - 1], to_lo(d)).wait_send()
        remote(low, low, h_send, h_recv.at[0], to_hi(1)).wait_send()
        for d in range(1, kn):
            spot = pack.at[d - 1]
            remote(spot, spot, y_send.at[d - 1], y_recv.at[d - 1, 0], to_kvh(d)).wait_send()
        gone = lambda count: remote(
            red.at[pl.ds(0, count)], red.at[pl.ds(0, count)], b_send, b_recv.at[0], to_core(1)
        ).wait_send()
        pl.when(kept_here)(lambda: gone(per - 1))
        pl.when(~kept_here)(lambda: gone(per))
        all_lines().wait_send()

        @pl.when(kept_here)
        def _():
            for d in range(1, kn):
                spot = blocks_got.at[pl.ds(0, per)]
                remote(spot, spot, f_send.at[d - 1], f_recv.at[0], to_kvh(d)).wait_send()

        for d in range(1, kn):
            square_copy(d).wait_send()

    b16 = jnp.bfloat16
    pl.run_scoped(
        attention_phase,
        pltpu.VMEM((heads, span, size), b16),
        pltpu.VMEM((heads, span, size), b16),
        pltpu.VMEM(wo_hbm.shape, b16),
        pltpu.VMEM((rows, span), jnp.float32),
        pltpu.VMEM((rows, nodes), jnp.float32),
        pltpu.VMEM((heads, rows, 2 * size), jnp.float32),
        pltpu.VMEM((heads, mine, wide), b16),
        pltpu.VMEM((n * mine, fb), jnp.float32),
    )
    pl.run_scoped(
        forward_phase,
        pltpu.VMEM((hs, width, 2 * hc), b16),
        pltpu.VMEM((3, hidden_width, fw), b16),
    )


def layer(
    queries, tree_keys, tree_values, keys, values, lengths, parents, residual, out_weight, norm_gain, gate_weight, up_weight,
    down_weight,
):
    dims = (*split_count(lax.axis_size("req")), lax.axis_size("ffn"))
    hn, ln, cn = dims
    kn = lax.axis_size("kvh")
    n = math.prod(dims)
    heads, span, size = keys.shape
    nodes, width = queries.shape
    wide = width // heads
    rows = wide // size * nodes
    mine, cols = residual.shape
    fb = out_weight.shape[1]
    hidden = gate_weight.shape[1]
    hc = lane_block(hidden, 256)
    fw = lane_block(cols, max(128, cols // 8))
    chunks = mine // ROWS
    items = chunks * cn
    tokens = n // cn * ROWS
    keep = tokens // kn
    steps = items * (hidden // hc)
    kept = chunks * (cols // fw)
    vmem = pl.BlockSpec(memory_space=pltpu.VMEM)
    hbm = pl.BlockSpec(memory_space=pl.ANY)
    f32, b16 = jnp.float32, jnp.bfloat16
    dma = pltpu.SemaphoreType.DMA
    return pl.pallas_call(
        functools.partial(layer_body, dims=dims, kn=kn, heads=heads, hc=hc, fw=fw),
        out_shape=jax.ShapeDtypeStruct(residual.shape, f32),
        in_specs=[
            pl.BlockSpec(memory_space=pltpu.SMEM), vmem, vmem, vmem, hbm, hbm, vmem, hbm, vmem, hbm, hbm, hbm, hbm,
        ],
        out_specs=vmem,
        scratch_shapes=[
            pltpu.VMEM((n * mine, width), b16),
            pltpu.VMEM((mine, cols), f32),
            pltpu.VMEM((mine, cols), b16),
            pltpu.VMEM((heads, cn - 1, rows // cn, 2 * size), f32),
            pltpu.VMEM((kn - 1, n // kn, mine, fb), b16),
            pltpu.VMEM((kn - 1, n // kn, mine, fb), b16),
            pltpu.VMEM((n // kn, mine, fb), b16),
            pltpu.VMEM((n, mine, fb), b16),
            pltpu.VMEM((n // kn, mine, fb), b16),
            pltpu.VMEM((mine, 128), f32),
            pltpu.VMEM((kn - 1, mine, 128), f32),
            pltpu.VMEM((8, 128), f32),
            pltpu.VMEM((n, 8, 128), f32),
            pltpu.VMEM((items, keep, 128), f32),
            pltpu.VMEM((BEHIND + 1, tokens, 2 * hc), f32),
            pltpu.VMEM((PARTS, kn - 1, keep, 2 * hc), b16),
            pltpu.VMEM((steps, kn - 1, keep, 2 * hc), b16),
            pltpu.VMEM((items, tokens, hidden), b16),
            pltpu.VMEM((cols // fw + 3, tokens, fw), f32),
            pltpu.VMEM((kept, cn - 1, tokens, fw), f32),
            pltpu.VMEM((kept, ln - 1, hn * ROWS, fw), b16),
            pltpu.VMEM((cols // fw, hn * ROWS, fw), f32),
            pltpu.VMEM((kept, ln - 1, hn * ROWS, fw), b16),
            pltpu.VMEM((kept, hn - 1, ROWS, fw), b16),
            pltpu.VMEM((kept, ROWS, fw), f32),
            pltpu.VMEM((kept, hn - 1, ROWS, fw), b16),
            dma((heads,)),
            dma((heads,)),
            dma,
            dma,
            dma((hidden // hc,)),
            dma((3,)),
            *gather_sems(heads, dims),
            *gather_sems(chunks, dims),
            dma((cn - 1,)),
            dma((heads, cn - 1)),
            dma((kn - 1,)),
            dma((kn - 1, n // kn)),
            dma,
            dma((n,)),
            dma((kn - 1,)),
            dma((n // kn,)),
            dma((kn - 1,)),
            dma((kn - 1,)),
            dma,
            dma,
            pltpu.SemaphoreType.REGULAR,
            dma((PARTS, kn - 1)),
            dma((3 * BEHIND, kn - 1)),
            dma((kn - 1,)),
            dma((items, kn - 1)),
            dma((cn - 1, 3)),
            dma((kept, cn - 1)),
            dma((ln - 1,)),
            dma((kept, ln - 1)),
            dma,
            dma((kept,)),
        ],
        compiler_params=pltpu.CompilerParams(collective_id=1, has_side_effects=True, vmem_limit_bytes=63 * 1024 * 1024),
    )(
        lengths, queries, tree_keys, tree_values, keys, values, parents, residual, norm_gain[None, :], out_weight,
        gate_weight, up_weight, down_weight,
    )


def local(
    queries, tree_keys, tree_token_values, cache_keys, cached_value_rows, lengths, parents, residual, out_weight, norm_gain,
    gate_weight, up_weight, down_weight,
):
    return layer(
        queries[0], tree_keys[0], tree_token_values[0], cache_keys[0], cached_value_rows[0], lengths, parents, residual,
        out_weight, norm_gain, gate_weight, up_weight, down_weight,
    )


def solution(mesh):
    in_specs = (
        P("req", None, "kvh"),
        P("req", None, "kvh"),
        P("req", None, "kvh"),
        P("req", "kvh", "ffn", None),
        P("req", "kvh", "ffn", None),
        P(),
        P("req", None),
        P(("req", "ffn"), "kvh"),
        P("kvh", ("req", "ffn")),
        P("kvh"),
        P("kvh", ("req", "ffn")),
        P("kvh", ("req", "ffn")),
        P(("req", "ffn"), "kvh"),
    )
    out_specs = P(("req", "ffn"), "kvh")
    return jax.shard_map(local, mesh=mesh, in_specs=in_specs, out_specs=out_specs, check_vma=False)
```
